256 devices in a mesh: req: 8 (over y_hi, x), blk: 32 (over y_lo, z, core).
Axes of the slice: x: 4, y: 4 (y_hi: 2, y_lo: 2; y = y_hi * 2 + y_lo), z: 8, core: 2. Of those that a mesh axis runs over, the one named last changes fastest.
Arguments:
- prefill_resid: bfloat16 [1024, 2048], P(('blk', 'req')), may hold values from -3 to 3
- prefill_routes: int32 [1024, 6], P(('blk', 'req')), may hold values from 0 to 63, all different within a row; in each aligned block of 32 rows (0 to 31, 32 to 63, ...) at most 6 rows name the same one
- prefill_scores: float32 [1024, 6], P(('blk', 'req')), may hold values from 0.05 to 1
- decode_resid: bfloat16 [16, 2048], P('req'), may hold values from -3 to 3
- queries: bfloat16 [16, 16, 192], P('req'), may hold values from -8 to 8
- latent_cache: bfloat16 [16, 16384, 576], P('req', 'blk'), may hold values from -8 to 8
- new_latent: bfloat16 [16, 576], P('req'), may hold values from -8 to 8
- cache_lengths: int32 [16], P('req'), may hold values from 1 to 16384, 65536 in all
- decode_routes: int32 [16, 6], P('req'), may hold values from 0 to 63, all different within a row
- decode_scores: float32 [16, 6], P('req'), may hold values from 0.05 to 1
- norm_gain: float32 [2048], replicated, may hold values from 0.1 to 1.9
- absorb_key: bfloat16 [16, 128, 512], replicated, may hold values from -0.5 to 0.5
- absorb_value: bfloat16 [16, 512, 128], P('req'), may hold values from -6 to 6
- out_proj: bfloat16 [16, 128, 2048], P('req'), may hold values from -0.125 to 0.125
- expert_gate: bfloat16 [64, 2048, 1408], P('blk', None, 'req'), may hold values from -0.125 to 0.125
- expert_up: bfloat16 [64, 2048, 1408], P('blk', None, 'req'), may hold values from -0.125 to 0.125
- expert_down: bfloat16 [64, 1408, 2048], P('blk', 'req'), may hold values from -0.15625 to 0.15625
- shared_gate: bfloat16 [2048, 2816], P(None, 'req'), may hold values from -0.125 to 0.125
- shared_up: bfloat16 [2048, 2816], P(None, 'req'), may hold values from -0.125 to 0.125
- shared_down: bfloat16 [2816, 2048], P('req'), may hold values from -0.109375 to 0.109375
Outputs:
- prefill_out: bfloat16 [1024, 2048], P(('blk', 'req'))
- decode_out: bfloat16 [16, 2048], P('req')
The draws below stay inside these ranges and needn't reach their ends.
Inputs may be any that keep to these rules, and one draw needn't show every extreme that they name: `prefill_routes`: each token names 6 different experts; every expert is named by some token; in each aligned block of 32 tokens no expert is named by more than 6 tokens, and in some block one expert is named by exactly 6. `decode_routes`: each decoded token names 6 different experts; every expert is named by some token. `cache_lengths`: some request has exactly 16384 cached positions.
All inputs are finite; a program needn't handle non-finite values. No bound on the sum of `cache_lengths` on one device may be relied on, other than what follows from the above.
Results may differ from the reference program's by a relative error of at most 0.02.
Values may be sent and summed in bfloat16 or wider, within the bound.
No kernel may reach another device: no remote copies, remote signals or barrier semaphores. Data moves between devices by JAX's collectives and lax.ppermute only.
A program may use at most 128 MiB of HBM per device.

```python
import math
import jax
import jax.numpy as jnp
import numpy as np
from jax import lax

D = 2048
HEADS = 16
NOPE = 128
ROPE = 64
VHEAD = 128
LATENT = 512
FF = 1408
SHARED = 2816
TOPK = 6
LMAX = 16384
PRE_DEV = 4
EXPERTS = 64
PRE = 1024
DECS = 16
PMOST = 6
N_REQ = 8


def draw_queries(key, part):
    drawn = jax.random.truncated_normal(jax.random.fold_in(key, 1), -6.0, 6.0, (DECS, HEADS, NOPE + ROPE), jnp.float32)
    return drawn.astype(jnp.bfloat16)


def draw_new_latent(key, part):
    latent_part = 2.0 * jax.random.truncated_normal(jax.random.fold_in(key, 2), -4.0, 4.0, (DECS, LATENT), jnp.float32)
    rotary = jax.random.truncated_normal(jax.random.fold_in(key, 3), -6.0, 6.0, (DECS, ROPE), jnp.float32)
    return jnp.concatenate([latent_part, rotary], axis=1).astype(jnp.bfloat16)


def draw_latent_cache(key, part):
    latent_part = 2.0 * jax.random.truncated_normal(jax.random.fold_in(key, 4), -4.0, 4.0, (DECS, LMAX, LATENT), jnp.float32)
    rotary = jax.random.truncated_normal(jax.random.fold_in(key, 5), -6.0, 6.0, (DECS, LMAX, ROPE), jnp.float32)
    return jnp.concatenate([latent_part, rotary], axis=2).astype(jnp.bfloat16)


def block_scale(own_key, extent, shards, low, high):
    def one(axis_at, shards_of):
        steps = jax.random.uniform(jax.random.fold_in(jax.random.fold_in(own_key, 6), axis_at), (shards_of,), jnp.float32, low / len(shards), high / len(shards))
        return jnp.repeat(jnp.exp(steps), extent[axis_at] // shards_of).reshape((-1,) + (1,) * (len(extent) - axis_at - 1))

    level = one(*shards[0])
    for cut in shards[1:]:
        level = level * one(*cut)
    return level


def different_ones(key, rows, amount, top, lift):
    sequence = jax.random.permutation(jax.random.fold_in(key, 1), amount)
    boost = sequence
    for power in range(3):
        boost = boost * boost // amount
    boost = boost * lift // amount
    chance = jax.random.randint(jax.random.fold_in(key, 2), (rows, amount), 0, 4096) + boost
    fixed_rows = jax.random.permutation(jax.random.fold_in(key, 3), rows)[jnp.arange(amount) % rows]
    chance = jnp.where(jnp.arange(rows)[:, None] == fixed_rows[None, :], 1 << 14, chance)
    score = chance * amount + jnp.arange(amount)
    return lax.top_k(score.astype(jnp.int32), top)[1].astype(jnp.int32)


def split_up(count, total, most, slope):
    weights = [(1 << 20) // math.isqrt(standing ** slope) + 1 for standing in range(2, count + 1)]
    surplus, given = total - most - (count - 1), [1] * (count - 1)
    while surplus > 0:
        free = [i for i in range(count - 1) if given[i] < most]
        pool, budget = sum([weights[i] for i in free]), surplus
        for i in free:
            addition = min(most - given[i], max(1, budget * weights[i] // pool), surplus)
            given[i] = given[i] + addition
            surplus = surplus - addition
    return np.array([most] + given)


def ragged_sizes(own_key, count, total, bound, slope):
    if count == 2:
        one = jax.random.randint(own_key, (), max(1, total - bound), min(bound, total - 1) + 1)
        return jnp.stack([one, total - one])
    sizes = jnp.asarray(split_up(count, total, bound, slope), jnp.int32)
    twos = (count - 1) // 2
    source_of, taker = sizes[1:1 + 2 * twos:2], sizes[2:2 + 2 * twos:2]
    slack = jnp.minimum(source_of - 1, bound - taker)
    passed = jax.random.randint(jax.random.fold_in(own_key, 1), (twos,), 0, 1 << 20) % (slack + 1)
    sizes = sizes.at[1:1 + 2 * twos:2].set(source_of - passed).at[2:2 + 2 * twos:2].set(taker + passed)
    return sizes[jax.random.permutation(jax.random.fold_in(own_key, 2), count)]


def deal_out(own_key, own, number, rows, number_of, top, bound, lean):
    order = jax.random.permutation(own_key, number_of)
    packed, usual = shares(number_of, rows * top, bound, lean, True), shares(number_of, rows * top, bound, lean, False)
    places = jnp.arange(number_of)

    def named(lengths, rotation):
        used = int((lengths > 0).sum())
        fixed = max(1, used // 4)
        passed = fixed + (places - fixed + rotation * (used - fixed)) % max(1, number_of - fixed)
        return jnp.zeros((number_of,), jnp.int32).at[order[jnp.where(places < fixed, places, passed)]].set(jnp.asarray(lengths, jnp.int32))

    lengths = jnp.where(number % 4 == 0, named(packed, number // 4), named(usual, number - number // 4 - 1))
    mixed = jax.random.permutation(jax.random.fold_in(own, 3), number_of)
    giver, sink = mixed[0:number_of // 2 * 2:2], mixed[1:number_of // 2 * 2:2]
    room = jnp.minimum(lengths[giver] - 1, bound - lengths[sink]) // 2
    room = jnp.where((giver == order[0]) | (sink == order[0]) | (lengths[sink] == 0), 0, jnp.maximum(room, 0))
    passed = jax.random.randint(jax.random.fold_in(own, 4), (number_of // 2,), 0, 1 << 20) % (room + 1)
    lengths = lengths.at[giver].add(-passed).at[sink].add(passed)
    labels = jnp.searchsorted(jnp.cumsum(lengths), jnp.arange(rows * top), side="right").astype(jnp.int32)
    table = labels.reshape(top, rows).T
    table = table[jax.random.permutation(jax.random.fold_in(own, 1), rows)]
    rotation = jax.random.randint(jax.random.fold_in(own, 2), (rows, 1), 0, top)
    return jnp.take_along_axis(table, (jnp.arange(top)[None, :] + rotation) % top, axis=1)


def shares(amount, total, reach, skew, full):
    portions = [(1 << 20) // math.isqrt(grade ** skew) + 1 for grade in range(1, amount + 1)]
    largest = reach if full else min(reach, max(-(-total // amount), total * portions[0] // sum(portions)))
    least = 1 if total - largest >= amount - 1 else 0
    holding, spare = [largest] + [least] * (amount - 1), total - largest - least * (amount - 1)
    while spare > 0:
        free = [i for i in range(1, amount) if holding[i] < largest] or [i for i in range(1, amount) if holding[i] < reach]
        whole, left = sum([portions[i] for i in free]), spare
        for i in free:
            addition = min(reach - holding[i], max(1, left * portions[i] // whole), spare)
            holding[i] = holding[i] + addition
            spare = spare - addition
    return np.array(holding)


def scatter_about(key, extent, width, reach, cuts=(), kind=jnp.bfloat16):
    entries = width * jax.random.normal(key, extent, jnp.float32)
    if cuts:
        entries = entries * block_scale(key, extent, cuts, -0.22, 0.18)
    return jnp.clip(entries, -reach, reach).astype(kind)


def setup_inputs(seed: int = 0) -> dict:
    arg_keys = jax.random.split(jax.random.key(seed), 21)
    prefill_resid = scatter_about(arg_keys[0], (PRE, D), 0.5, 3.0, ((0, 256),))
    prefill_routes_keys = jax.random.split(jax.random.fold_in(arg_keys[1], 1), PRE // (N_REQ * PRE_DEV))
    prefill_routes_turns = jax.random.permutation(jax.random.fold_in(arg_keys[1], 3), PRE // (N_REQ * PRE_DEV))
    prefill_routes = jax.vmap(lambda own, number: deal_out(jax.random.fold_in(arg_keys[1], 2), own, number, N_REQ * PRE_DEV, EXPERTS, TOPK, PMOST, 2))(prefill_routes_keys, prefill_routes_turns).reshape((PRE, TOPK))
    prefill_scores = jnp.clip(jnp.exp(math.log(1.0) - 2.9957323 * jax.random.uniform(arg_keys[2], (PRE, TOPK), jnp.float32) ** block_scale(arg_keys[2], (PRE, TOPK), ((0, 256),), -0.2, 0.2)), 0.05, 1.0)
    decode_resid = scatter_about(arg_keys[3], (DECS, D), 0.5, 3.0, ((0, 8),))
    queries = draw_queries(jax.random.fold_in(arg_keys[20], 71), 0)
    latent_cache = draw_latent_cache(jax.random.fold_in(arg_keys[20], 71), 0)
    new_latent = draw_new_latent(jax.random.fold_in(arg_keys[20], 71), 0)
    cache_lengths = ragged_sizes(arg_keys[7], DECS, DECS * LMAX // 4, LMAX, 2).astype(jnp.int32)
    decode_routes = different_ones(arg_keys[8], DECS, EXPERTS, TOPK, 1536)
    decode_scores = jnp.clip(jnp.exp(math.log(1.0) - 2.9957323 * jax.random.uniform(arg_keys[9], (DECS, TOPK), jnp.float32) ** block_scale(arg_keys[9], (DECS, TOPK), ((0, 8),), -0.2, 0.2)), 0.05, 1.0)
    norm_gain = jnp.clip(1.0 + 0.18 * jax.random.normal(arg_keys[10], (D,), jnp.float32), 0.1, 1.9)
    absorb_key = scatter_about(arg_keys[11], (HEADS, NOPE, LATENT), NOPE ** -0.5, 0.5)
    absorb_value = scatter_about(arg_keys[12], (HEADS, LATENT, VHEAD), 1.0, 6.0, ((0, 8),))
    out_proj = scatter_about(arg_keys[13], (HEADS, VHEAD, D), (HEADS * VHEAD) ** -0.5, 0.125, ((0, 8),))
    expert_gate = scatter_about(arg_keys[14], (EXPERTS, D, FF), D ** -0.5, 0.125, ((0, 32), (2, 8)))
    expert_up = scatter_about(arg_keys[15], (EXPERTS, D, FF), D ** -0.5, 0.125, ((0, 32), (2, 8)))
    expert_down = scatter_about(arg_keys[16], (EXPERTS, FF, D), FF ** -0.5, 0.15625, ((0, 32), (1, 8)))
    shared_gate = scatter_about(arg_keys[17], (D, SHARED), D ** -0.5, 0.125, ((1, 8),))
    shared_up = scatter_about(arg_keys[18], (D, SHARED), D ** -0.5, 0.125, ((1, 8),))
    shared_down = scatter_about(arg_keys[19], (SHARED, D), SHARED ** -0.5, 0.109375, ((0, 8),))
    return {"prefill_resid": prefill_resid, "prefill_routes": prefill_routes, "prefill_scores": prefill_scores, "decode_resid": decode_resid, "queries": queries, "latent_cache": latent_cache, "new_latent": new_latent, "cache_lengths": cache_lengths, "decode_routes": decode_routes, "decode_scores": decode_scores, "norm_gain": norm_gain, "absorb_key": absorb_key, "absorb_value": absorb_value, "out_proj": out_proj, "expert_gate": expert_gate, "expert_up": expert_up, "expert_down": expert_down, "shared_gate": shared_gate, "shared_up": shared_up, "shared_down": shared_down}


NEG = -1e+30
ROUTE_SCALE = 2.446

def settle(values):
    return lax.optimization_barrier(values.astype(jnp.bfloat16)).astype(jnp.float32)

def rms_rows(rows_in, gain_row):
    widened = rows_in.astype(jnp.float32)
    mean_square = lax.optimization_barrier(jnp.mean(widened * widened, axis=1, keepdims=True))
    return (widened * lax.rsqrt(mean_square + 1e-06) * gain_row).astype(jnp.bfloat16)

def swiglu(inputs, gate_w, up_w, down_w):
    gate_part = jnp.dot(inputs, gate_w, preferred_element_type=jnp.float32)
    up_part = jnp.dot(inputs, up_w, preferred_element_type=jnp.float32)
    hidden = (jax.nn.silu(gate_part) * up_part).astype(jnp.bfloat16)
    return jnp.dot(hidden, down_w, preferred_element_type=jnp.float32)

def route_shares(scores):
    return scores / lax.optimization_barrier(jnp.sum(scores, axis=1, keepdims=True)) * ROUTE_SCALE

def routed_moe(normed, routes, slot_gains, expert_gate, expert_up, expert_down):
    tile_size = 64
    token_count = normed.shape[0]
    slot_count = token_count * TOPK
    flat_expert = routes.reshape(-1).astype(jnp.int32)
    flat_token = (jnp.arange(slot_count, dtype=jnp.int32) // TOPK).astype(jnp.int32)
    flat_gain = slot_gains.reshape(-1).astype(jnp.float32)
    onehot = (flat_expert[:, None] == jnp.arange(EXPERTS, dtype=jnp.int32)[None, :]).astype(jnp.int32)
    counts = lax.optimization_barrier(jnp.sum(onehot, axis=0))
    padded = (counts + tile_size - 1) // tile_size * tile_size
    group_ends = jnp.cumsum(padded)
    starts = group_ends - padded
    earlier = lax.optimization_barrier(jnp.sum((jnp.cumsum(onehot, axis=0) - onehot) * onehot, axis=1))
    targets = (starts[flat_expert] + earlier).astype(jnp.int32)
    capacity = (slot_count // tile_size + 1 + EXPERTS) * tile_size
    token_at = jnp.zeros((capacity,), jnp.int32).at[targets].set(flat_token)
    gain_at = jnp.zeros((capacity,), jnp.float32).at[targets].set(flat_gain)
    tile_count = capacity // tile_size
    tile_first = jnp.arange(tile_count, dtype=jnp.int32) * tile_size
    tile_expert = jnp.minimum(lax.optimization_barrier(jnp.sum((group_ends[None, :] <= tile_first[:, None]).astype(jnp.int32), axis=1)), EXPERTS - 1).astype(jnp.int32)

    def one_tile(running, tile_index):
        row_ids = lax.dynamic_slice_in_dim(token_at, tile_index * tile_size, tile_size)
        row_gain = lax.dynamic_slice_in_dim(gain_at, tile_index * tile_size, tile_size)
        chosen = tile_expert[tile_index]
        outputs = swiglu(normed[row_ids], expert_gate[chosen], expert_up[chosen], expert_down[chosen])
        return (running.at[row_ids].add(outputs * row_gain[:, None]), None)
    start_sum = jnp.zeros((token_count, normed.shape[1]), jnp.float32)
    return lax.scan(one_tile, start_sum, jnp.arange(tile_count, dtype=jnp.int32))[0]

def reference(prefill_resid, prefill_routes, prefill_scores, decode_resid, queries, latent_cache, new_latent, cache_lengths, decode_routes, decode_scores, norm_gain, absorb_key, absorb_value, out_proj, expert_gate, expert_up, expert_down, shared_gate, shared_up, shared_down):
    scale_factor = (NOPE + ROPE) ** (-0.5)

    def attend(items):
        query_row, cached, fresh_latent, length = items
        q_latent = jnp.einsum('hn,hnl->hl', query_row[:, :NOPE].astype(jnp.float32), absorb_key.astype(jnp.float32)).astype(jnp.bfloat16)
        q_full = jnp.concatenate([q_latent, query_row[:, NOPE:]], axis=1)
        scores = jnp.dot(q_full, cached.T, preferred_element_type=jnp.float32) * scale_factor
        live_mask = jnp.arange(LMAX, dtype=jnp.int32)[None, :] < length
        scores = jnp.where(live_mask, scores, NEG)
        fresh_score = jnp.dot(q_full, fresh_latent, preferred_element_type=jnp.float32) * scale_factor
        row_peak = jnp.maximum(lax.optimization_barrier(jnp.max(scores, axis=1)), fresh_score)
        expo_weights = jnp.where(live_mask, jnp.exp(scores - row_peak[:, None]), 0.0)
        fresh_weight = jnp.exp(fresh_score - row_peak)
        denominator = lax.optimization_barrier(jnp.sum(expo_weights, axis=1)) + fresh_weight
        weighted = jnp.dot(expo_weights.astype(jnp.bfloat16), cached[:, :LATENT], preferred_element_type=jnp.float32)
        weighted = weighted + settle(fresh_weight)[:, None] * fresh_latent[None, :LATENT].astype(jnp.float32)
        o_latent = (weighted / denominator[:, None]).astype(jnp.bfloat16)
        head_values = jnp.einsum('hl,hlv->hv', o_latent.astype(jnp.float32), absorb_value.astype(jnp.float32)).astype(jnp.bfloat16)
        return jnp.einsum('hv,hvd->d', head_values.astype(jnp.float32), out_proj.astype(jnp.float32))
    attention = lax.map(attend, (queries, latent_cache, new_latent, cache_lengths))
    hidden_dec = (decode_resid.astype(jnp.float32) + attention).astype(jnp.bfloat16)
    resid_rows = jnp.concatenate([prefill_resid, hidden_dec], axis=0)
    normed = rms_rows(resid_rows, norm_gain)
    routes = jnp.concatenate([prefill_routes, decode_routes], axis=0)
    slot_gains = route_shares(jnp.concatenate([prefill_scores, decode_scores], axis=0)).astype(jnp.bfloat16)
    expert_sum = routed_moe(normed, routes, slot_gains, expert_gate, expert_up, expert_down)
    expert_sum = expert_sum + swiglu(normed, shared_gate, shared_up, shared_down)
    outputs = (resid_rows.astype(jnp.float32) + expert_sum).astype(jnp.bfloat16)
    return (outputs[:PRE], outputs[PRE:])
```

```python
import jax
import jax.numpy as jnp
from jax import lax
from jax.sharding import PartitionSpec as P

NEG = -1e30
ROUTE_SCALE = 2.446
CAP = 6
BF = jnp.bfloat16
F32 = jnp.float32


def exchange(payload, axis):
    return lax.all_to_all(payload, axis, 0, 0, tiled=True)


def pieces(values, count):
    parts, rest = [], values
    for _ in range(count):
        part = lax.reduce_precision(rest, 8, 7)
        parts.append(part.astype(BF))
        rest = rest - part
    return parts


def rms_rows(rows_in, gain_row):
    widened = rows_in.astype(F32)
    mean_square = jnp.mean(widened * widened, axis=1, keepdims=True)
    return (widened * lax.rsqrt(mean_square + 1e-06) * gain_row).astype(BF)


def dot(a, b):
    return jnp.dot(a, b, preferred_element_type=F32)


def swiglu(inputs, gate_w, up_w, down_w):
    hidden = (jax.nn.silu(dot(inputs, gate_w)) * dot(inputs, up_w)).astype(BF)
    return dot(hidden, down_w)


def route_row(routes, scores):
    shares = scores / jnp.sum(scores, axis=1, keepdims=True) * ROUTE_SCALE
    return jnp.concatenate([routes.astype(BF), shares.astype(BF)], axis=1)


def widen(values, width):
    return jnp.pad(values, [(0, 0)] * (values.ndim - 1) + [(0, width - values.shape[-1])])


def route_tables(rows, top, experts):
    matches = rows[:, :top].astype(jnp.int32)[:, :, None] == jnp.arange(experts, dtype=jnp.int32)
    named = jnp.sum(matches.astype(F32), axis=1)
    weight = jnp.sum(jnp.where(matches, rows[:, top : 2 * top].astype(F32)[:, :, None], 0.0), axis=1)
    return named, weight


def local(
    prefill_resid,
    prefill_routes,
    prefill_scores,
    decode_resid,
    queries,
    latent_cache,
    new_latent,
    cache_lengths,
    decode_routes,
    decode_scores,
    norm_gain,
    absorb_key,
    absorb_value,
    out_proj,
    expert_gate,
    expert_up,
    expert_down,
    shared_gate,
    shared_up,
    shared_down,
):
    req_n = lax.axis_size("req")
    blk_n = lax.axis_size("blk")
    r = lax.axis_index("req")
    b = lax.axis_index("blk")
    top = prefill_routes.shape[1]
    width = prefill_resid.shape[1]
    slice_w = width // req_n
    pre_n = prefill_resid.shape[0]
    col_n = pre_n * req_n
    own_req = decode_resid.shape[0]
    heads = queries.shape[1]
    own_heads = heads // req_n
    nope = absorb_key.shape[1]
    latent = absorb_key.shape[2]
    positions = latent_cache.shape[1]
    own_exp = expert_gate.shape[0]
    experts = own_exp * blk_n
    scale = queries.shape[2] ** (-0.5)
    part_w = latent + 128

    q_latent = jnp.einsum(
        "ihn,hnl->ihl", queries[:, :, :nope], absorb_key, preferred_element_type=F32
    ).astype(BF)
    q_full = jnp.concatenate([q_latent, queries[:, :, nope:]], axis=2)
    live = (b * positions + jnp.arange(positions, dtype=jnp.int32))[None, :] < cache_lengths[:, None]
    scores = jnp.einsum("ihc,ipc->ihp", q_full, latent_cache, preferred_element_type=F32) * scale
    scores = jnp.where(live[:, None, :], scores, NEG)
    fresh = jnp.einsum("ihc,ic->ih", q_full, new_latent, preferred_element_type=F32) * scale
    fresh = jnp.where(b == 0, fresh, NEG)
    peak = jnp.maximum(jnp.max(scores, axis=2), fresh)
    expo = jnp.where(live[:, None, :], jnp.exp(scores - peak[:, :, None]), 0.0)
    fresh_w = jnp.where(b == 0, jnp.exp(fresh - peak), 0.0)
    total = jnp.sum(expo, axis=2) + fresh_w
    summed = jnp.einsum(
        "ihp,ipl->ihl", expo.astype(BF), latent_cache[:, :, :latent], preferred_element_type=F32
    ) + fresh_w[:, :, None] * new_latent[:, None, :latent].astype(F32)
    mean = (summed / jnp.where(total > 0, total, 1.0)[:, :, None]).astype(BF)
    stats = jnp.stack(pieces(peak, 3) + pieces(total, 3), axis=-1)
    part = widen(jnp.concatenate([mean, stats], axis=-1), part_w)

    pre_row = jnp.concatenate(
        [rms_rows(prefill_resid, norm_gain), widen(route_row(prefill_routes, prefill_scores), 128)], 1
    )
    att_row = part.reshape(own_req, req_n, own_heads * part_w).transpose(1, 0, 2)
    dec_meta = jnp.broadcast_to(
        route_row(decode_routes, decode_scores)[None], (req_n, own_req, 2 * top)
    )
    att_row = widen(jnp.concatenate([att_row, dec_meta], axis=2), width + 128)
    sent = jnp.concatenate(
        [jnp.broadcast_to(pre_row[None], (req_n,) + pre_row.shape), att_row], axis=1
    )
    got = exchange(sent, "req")
    col_rows = got[:, :pre_n, :width].reshape(col_n, width)
    named, weight = route_tables(got[:, :pre_n, width:].reshape(col_n, 128), top, experts)
    pairs = got[:, pre_n:, : own_heads * part_w].reshape(blk_n, part_w)
    meta_at = own_heads * part_w
    dec_named, dec_weight = route_tables(
        got[:, pre_n:, meta_at : meta_at + 2 * top].reshape(req_n * own_req, 2 * top), top, experts
    )

    earlier = jnp.tril(jnp.ones((col_n, col_n), F32), -1)
    rank = dot(earlier, named)
    chosen = jnp.logical_and(
        named.T[:, None, :] > 0, rank.T[:, None, :] == jnp.arange(CAP, dtype=F32)[None, :, None]
    )
    mine = lax.dynamic_slice_in_dim(col_rows, r * slice_w, slice_w, 1)
    slots = jnp.einsum("est,tf->esf", chosen.astype(BF), mine, preferred_element_type=F32).astype(BF)
    sent = jnp.concatenate(
        [
            slots.reshape(blk_n, own_exp * CAP, slice_w),
            widen(pairs, 4 * slice_w).reshape(blk_n, 4, slice_w),
        ],
        axis=1,
    )
    got = exchange(sent, "blk")
    n_slot = own_exp * CAP
    slots = got[:, :n_slot].reshape(blk_n, own_exp, CAP, slice_w).transpose(1, 0, 2, 3)
    slots = slots.reshape(blk_n * n_slot, slice_w)
    part = got[:, n_slot:].reshape(blk_n, 4 * slice_w)
    peak = jnp.sum(part[:, latent : latent + 3].astype(F32), axis=1)
    total = jnp.sum(part[:, latent + 3 : latent + 6].astype(F32), axis=1)
    share = total * jnp.exp(peak - jnp.max(peak))
    o_latent = jnp.sum(share[:, None] * part[:, :latent].astype(F32), axis=0) / jnp.sum(share)
    head = b % own_heads
    request = b // own_heads
    head_value = dot(o_latent.astype(BF)[None], lax.dynamic_index_in_dim(absorb_value, head, 0, False))
    projected = dot(head_value.astype(BF), lax.dynamic_index_in_dim(out_proj, head, 0, False))[0]
    resid = lax.dynamic_index_in_dim(decode_resid, request % own_req, 0, False).astype(F32)
    owner = jnp.logical_and(request // own_req == r, head == 0)
    projected = projected + jnp.where(owner, resid, 0.0)

    sent = jnp.concatenate(
        [slots] + [p.reshape(req_n, slice_w) for p in pieces(projected, 2)], axis=0
    )
    got = exchange(jnp.broadcast_to(sent[None], (req_n,) + sent.shape), "req")
    n_all = blk_n * n_slot
    expert_rows = got[:, :n_all].transpose(1, 0, 2).reshape(own_exp, n_all // own_exp, width)
    projected = jnp.sum(got[:, n_all:].astype(F32).reshape(2 * req_n, width), axis=0)

    sent = jnp.stack(pieces(projected, 2))
    got = exchange(jnp.broadcast_to(sent[None], (blk_n,) + sent.shape), "blk")
    hidden_dec = jnp.sum(
        got.astype(F32).reshape(blk_n // own_heads, 2 * own_heads, width), axis=1
    ).astype(BF)
    dec_n = hidden_dec.shape[0]
    dec_rows = rms_rows(hidden_dec, norm_gain)

    shared_out = swiglu(
        jnp.concatenate([col_rows, dec_rows], axis=0), shared_gate, shared_up, shared_down
    )
    mask = jnp.logical_and(jnp.arange(dec_n) == request, head == 0)
    dec_sum = jnp.where(mask[:, None], shared_out[col_n:], 0.0)
    routed = []
    for k in range(own_exp):
        outs = swiglu(
            jnp.concatenate([expert_rows[k], dec_rows], axis=0),
            expert_gate[k],
            expert_up[k],
            expert_down[k],
        )
        routed.append(outs[: n_all // own_exp])
        dec_sum = dec_sum + outs[n_all // own_exp :] * lax.dynamic_slice_in_dim(
            dec_weight, b * own_exp + k, 1, 1
        )

    rows = jnp.concatenate(routed + [shared_out[:col_n]], axis=0).astype(BF)
    sent = jnp.concatenate(
        [
            rows.reshape(rows.shape[0], req_n, slice_w).transpose(1, 0, 2),
            dec_sum.astype(BF).reshape(req_n, own_req * req_n, slice_w),
        ],
        axis=1,
    )
    got = jnp.sum(exchange(sent, "req").astype(F32), axis=0)
    shared_col = got[n_all : n_all + col_n]

    back = got[:n_all].astype(BF).reshape(own_exp, blk_n, CAP, slice_w).transpose(1, 0, 2, 3)
    dec_part = got[n_all + col_n :].astype(BF)
    sent = jnp.concatenate(
        [
            back.reshape(blk_n, n_slot, slice_w),
            jnp.broadcast_to(dec_part[None], (blk_n,) + dec_part.shape),
        ],
        axis=1,
    )
    got = exchange(sent, "blk")
    dec_total = jnp.sum(got[:, n_slot:].astype(F32), axis=0).reshape(own_req, width)
    table = jnp.where(chosen, weight.T[:, None, :], 0.0).astype(BF)
    col_sum = shared_col + jnp.einsum(
        "est,esf->tf",
        table,
        got[:, :n_slot].reshape(experts, CAP, slice_w),
        preferred_element_type=F32,
    )

    got = exchange(col_sum.reshape(req_n, pre_n, slice_w), "req")
    own_sum = got.transpose(1, 0, 2).reshape(pre_n, width)
    prefill_out = (prefill_resid.astype(F32) + own_sum).astype(BF)
    own_dec = lax.dynamic_slice_in_dim(hidden_dec, r * own_req, own_req, 0)
    decode_out = (own_dec.astype(F32) + dec_total).astype(BF)
    return (prefill_out, decode_out)


def solution(mesh):
    return jax.shard_map(
        local,
        mesh=mesh,
        in_specs=(
            P(("blk", "req"), None),
            P(("blk", "req"), None),
            P(("blk", "req"), None),
            P("req", None),
            P("req", None, None),
            P("req", "blk", None),
            P("req", None),
            P("req"),
            P("req", None),
            P("req", None),
            P(),
            P(),
            P("req", None, None),
            P("req", None, None),
            P("blk", None, "req"),
            P("blk", None, "req"),
            P("blk", "req", None),
            P(None, "req"),
            P(None, "req"),
            P("req", None),
        ),
        out_specs=(P(("blk", "req"), None), P("req", None)),
        check_vma=False,
    )
```

```python
import jax
import jax.numpy as jnp
from jax import lax
from jax.experimental import pallas as pl
from jax.experimental.pallas import tpu as pltpu
from jax.sharding import PartitionSpec as P

NEG = -1e30
ROUTE_SCALE = 2.446
CAP = 6
BF = jnp.bfloat16
F32 = jnp.float32
I32 = jnp.int32
VMEM = pl.BlockSpec(memory_space=pltpu.VMEM)
SMEM = pl.BlockSpec(memory_space=pltpu.SMEM)


def exchange(payload, axis):
    return lax.all_to_all(payload, axis, 0, 0, tiled=True)


def dot(a, b):
    return jnp.dot(a, b, preferred_element_type=F32)


def dot_t(a, b):
    return lax.dot_general(a, b, (((1,), (1,)), ((), ())), preferred_element_type=F32)


def iota(shape, dim):
    return lax.broadcasted_iota(I32, shape, dim)


def bits(mask):
    return jnp.where(mask, 1.0, 0.0).astype(BF)


def rounded(values):
    return values.astype(BF).astype(F32)


def pieces(values):
    first = rounded(values)
    second = rounded(values - first)
    return [first, second, values - first - second]


def silu_mul(gate, up):
    return (gate * jax.nn.sigmoid(gate) * up).astype(BF)


def slot_of(row):
    place = row & 15
    second = (place >= CAP).astype(I32)
    return row >> 4, place, second, place - CAP * second


def start_kernel(*refs):
    count = (len(refs) - 2) // 2
    sources, out_ref, held, sems = refs[:count], refs[count], refs[count + 1 : -1], refs[-1]
    copies = [pltpu.make_async_copy(s, h, sems.at[n]) for n, (s, h) in enumerate(zip(sources, held))]
    for copy in copies:
        copy.start()
    q_ref, key_ref, res_ref, gain_ref, prt_ref, psc_ref, drt_ref, dsc_ref, new_ref, len_ref, cache_ref = held
    b = lax.axis_index("blk")
    for copy in copies[2:8]:
        copy.wait()
    pre_n, width = res_ref.shape
    n_req, heads, qw = q_ref.shape
    _, nope, latent = key_ref.shape
    positions = cache_ref.shape[2]
    scale = qw ** (-0.5)

    x = res_ref[...].astype(F32)
    mean_square = jnp.mean(x * x, axis=1, keepdims=True)
    rows = x * lax.rsqrt(mean_square + 1e-06) * gain_ref[...]

    def shares(sc):
        return rounded(sc / jnp.sum(sc, axis=1, keepdims=True) * ROUTE_SCALE)

    lane = iota((pre_n, 128), 1)
    row = iota((pre_n, 128), 0)
    top = prt_ref.shape[1]
    pr, ps = prt_ref[...].astype(F32), shares(psc_ref[...])
    dr, ds = drt_ref[...].astype(F32), shares(dsc_ref[...])
    meta = jnp.zeros((pre_n, 128), F32)
    for k in range(top):
        meta = jnp.where(lane == k, pr[:, k : k + 1], meta)
        meta = jnp.where(lane == top + k, ps[:, k : k + 1], meta)
        for i in range(n_req):
            at = jnp.logical_and(row == 2 * i, lane == 16 + k)
            meta = jnp.where(at, dr[i : i + 1, k : k + 1], meta)
            at = jnp.logical_and(row == 2 * i, lane == 16 + top + k)
            meta = jnp.where(at, ds[i : i + 1, k : k + 1], meta)

    for copy in copies[:2]:
        copy.wait()
    q_all = jnp.concatenate([q_ref[i] for i in range(n_req)], axis=0)
    q_nope = q_all[:, :nope]
    q_rope = q_all[:, nope:]
    q_head = iota((n_req * heads, latent), 0) & (heads - 1)
    q_lat = jnp.zeros((n_req * heads, latent), F32)
    for h in range(heads):
        q_lat = jnp.where(q_head == h, dot(q_nope, key_ref[h]), q_lat)
    q_lat = q_lat.astype(BF)

    for copy in copies[8:]:
        copy.wait()
    fresh_rows = new_ref[...].astype(F32)
    first = b == 0
    parts = []
    for i in range(n_req):
        ql = q_lat[i * heads : (i + 1) * heads]
        qr = q_rope[i * heads : (i + 1) * heads]
        s = (dot(ql, cache_ref[i, :latent, :]) + dot(qr, cache_ref[i, latent:, :])) * scale
        live = b * positions + iota((heads, positions), 1) < len_ref[i]
        s = jnp.where(live, s, NEG)
        new = fresh_rows[i : i + 1]
        fresh = jnp.sum(ql.astype(F32) * new[:, :latent], axis=1, keepdims=True)
        fresh = (fresh + jnp.sum(qr.astype(F32) * new[:, latent:], axis=1, keepdims=True)) * scale
        fresh = jnp.where(first, fresh, NEG)
        peak = jnp.maximum(jnp.max(s, axis=1, keepdims=True), fresh)
        expo = jnp.where(live, jnp.exp(s - peak), 0.0)
        fresh_w = jnp.where(first, jnp.exp(fresh - peak), 0.0)
        total = jnp.sum(expo, axis=1, keepdims=True) + fresh_w
        summed = dot_t(expo.astype(BF), cache_ref[i, :latent, :]) + rounded(fresh_w) * new[:, :latent]
        mean = summed / jnp.where(total > 0.0, total, 1.0)
        lane_h = iota((heads, 128), 1)
        stats = jnp.zeros((heads, 128), F32)
        for k, piece in enumerate(pieces(peak) + pieces(total)):
            stats = jnp.where(lane_h == k, piece, stats)
        parts.append(jnp.concatenate([mean, stats], axis=1))

    own = heads // out_ref.shape[0]
    for d in range(out_ref.shape[0]):
        att = jnp.concatenate([p[own * d : own * (d + 1)] for p in parts], axis=0)
        out_ref[d] = jnp.concatenate([rows, meta, att], axis=1).astype(BF)


def route_kernel(got_ref, send_ref, cols_ref, comb_ref, decw_ref):
    r = lax.axis_index("req")
    b = lax.axis_index("blk")
    n_src, pre_n, _ = got_ref.shape
    col_n, width = cols_ref.shape
    slice_w = send_ref.shape[2]
    blk_n = send_ref.shape[0]
    experts = 2 * blk_n
    top = 6
    full = jnp.concatenate([got_ref[s].astype(F32) for s in range(n_src)], axis=0)
    cols_ref[...] = full[:, :width].astype(BF)
    meta = full[:, width : width + 128]
    pairs = full[:, width + 128 :]

    expert = iota((col_n, experts), 1).astype(F32)
    named = jnp.zeros((col_n, experts), F32)
    weight = jnp.zeros((col_n, experts), F32)
    for k in range(top):
        hit = meta[:, k : k + 1] == expert
        named = jnp.where(hit, 1.0, named)
        weight = jnp.where(hit, meta[:, top + k : top + k + 1], weight)
    earlier = bits(iota((col_n, col_n), 1) < iota((col_n, col_n), 0))
    rank = dot(earlier, named.astype(BF))
    value = jnp.where(named > 0.0, rank + 1.0, 0.0)

    n_row = blk_n * 16
    column, place, second, slot = slot_of(iota((n_row, experts), 0))
    picks = jnp.logical_and(iota((n_row, experts), 1) == 2 * column + second, place < 2 * CAP)
    picks = bits(picks)
    rest = jnp.zeros((128 - col_n, experts), F32)
    value = dot_t(picks, jnp.concatenate([value, rest], axis=0).astype(BF))
    weight = dot_t(picks, jnp.concatenate([weight, rest], axis=0).astype(BF))
    row = iota((n_row, 128), 0)
    lane = iota((n_row, 128), 1)
    _, _, _, slot = slot_of(row)
    chosen = value == (slot + 1).astype(F32)
    comb_ref[...] = jnp.where(chosen, weight, 0.0).astype(BF)
    carried = jnp.logical_and(lane >= col_n, row == (lane & (col_n - 1)) * 16 + 11 + (lane >> 5))
    mine = cols_ref[:, pl.ds(pl.multiple_of(r * slice_w, slice_w), slice_w)]
    last = jnp.concatenate([pairs[:, 2 * slice_w :], jnp.zeros((col_n, slice_w - 128), F32)], axis=1)
    data = jnp.concatenate(
        [mine, pairs[:, :slice_w].astype(BF), pairs[:, slice_w : 2 * slice_w].astype(BF), last.astype(BF)],
        axis=0,
    )
    moved = dot(bits(jnp.logical_or(chosen, carried)), data).astype(BF)
    send_ref[...] = moved.reshape(send_ref.shape)

    lane = iota((col_n, 128), 1)
    dec = jnp.zeros((col_n, 128), F32)
    for k in range(2):
        own = (2 * b + k).astype(F32)
        got = jnp.zeros((col_n, 1), F32)
        for j in range(top):
            hit = meta[:, 16 + j : 17 + j] == own
            got = jnp.where(hit, meta[:, 16 + top + j : 17 + top + j], got)
        dec = jnp.where(lane == k, got, dec)
    even = bits(iota((col_n // 2, col_n), 1) == 2 * iota((col_n // 2, col_n), 0))
    decw_ref[...] = dot(even, dec.astype(BF))


def head_kernel(got_ref, val_ref, proj_ref, res_ref, send_ref):
    r = lax.axis_index("req")
    b = lax.axis_index("blk")
    n_src, block, slice_w = got_ref.shape
    n_dst, n_out, _ = send_ref.shape
    n_slot = n_out - 8
    half = n_slot // 2
    got = got_ref[...].reshape(n_src * block, slice_w)
    column, place, second, slot = slot_of(iota((n_slot, n_src * block), 1))
    target = second * half + column * CAP + slot
    keep = jnp.logical_and(iota((n_slot, n_src * block), 0) == target, place < 2 * CAP)
    slots = dot(bits(keep), got).astype(BF)
    for d in range(n_dst):
        send_ref[d, :n_slot, :] = slots

    line = iota((3 * n_src, n_src * block), 0)
    part = iota((3 * n_src, n_src * block), 1) == (line & (n_src - 1)) * block + 12 + (line >> 5)
    part = dot(bits(part), got)
    stats = part[2 * n_src :]
    peak = stats[:, 0:1] + stats[:, 1:2] + stats[:, 2:3]
    total = stats[:, 3:4] + stats[:, 4:5] + stats[:, 5:6]
    share = total * jnp.exp(peak - jnp.max(peak, axis=0, keepdims=True))
    whole = jnp.sum(share, axis=0, keepdims=True)
    low = jnp.sum(part[:n_src] * share, axis=0, keepdims=True) / whole
    high = jnp.sum(part[n_src : 2 * n_src] * share, axis=0, keepdims=True) / whole
    o_latent = jnp.broadcast_to(jnp.concatenate([low, high], axis=1), (8, 2 * slice_w)).astype(BF)
    head = b & 1
    request = b >> 1
    head_value = dot(o_latent, val_ref[head]).astype(BF)
    projected = dot(head_value, proj_ref[head])[0:1]
    resid = res_ref[...].astype(F32)
    resid = jnp.where(iota(resid.shape, 0) == (request & 1), resid, 0.0)
    resid = jnp.sum(resid, axis=0, keepdims=True)
    owner = jnp.logical_and(request >> 1 == r, head == 0)
    projected = projected + jnp.where(owner, resid, 0.0)
    folded = jnp.concatenate(
        [projected[:, slice_w * j : slice_w * (j + 1)] for j in range(8)], axis=0
    ).astype(BF)
    for d in range(n_dst):
        send_ref[d, n_slot:, :] = folded


def sum_kernel(got_ref, send_ref):
    n_src, n_all, _ = got_ref.shape
    total = got_ref[0, n_all - 8 :, :].astype(F32)
    for s in range(1, n_src):
        total = total + got_ref[s, n_all - 8 :, :].astype(F32)
    total = total.astype(BF)
    for d in range(send_ref.shape[0]):
        send_ref[d] = total


def terms_kernel(
    got_ref,
    rows_ref,
    cols_ref,
    gain_ref,
    decw_ref,
    gate_ref,
    up_ref,
    down_ref,
    sg_ref,
    su_ref,
    sd_ref,
    out_ref,
    shared_ref,
    hid_ref,
):
    b = lax.axis_index("blk")
    n_src, fold, slice_w = got_ref.shape
    dec_n = n_src // 2
    n_line = fold * dec_n
    got = got_ref[...].reshape(n_src * fold, slice_w)
    line = iota((n_line, n_src * fold), 0)
    col = iota((n_line, n_src * fold), 1)
    pick = jnp.logical_and(col >> 4 == (line & (dec_n - 1)), (col & 7) == line >> 4)
    hidden = dot(bits(pick), got).astype(BF)
    wide = hidden.astype(F32)
    chunks = [wide[j * dec_n : (j + 1) * dec_n] for j in range(fold)]
    square = sum(jnp.sum(c * c, axis=1, keepdims=True) for c in chunks)
    factor = lax.rsqrt(square / (fold * slice_w) + 1e-06)
    normed = [
        (c * factor * gain_ref[:, j * slice_w : (j + 1) * slice_w]).astype(BF)
        for j, c in enumerate(chunks)
    ]

    col_n = cols_ref.shape[0]
    x = jnp.concatenate([cols_ref[...], jnp.concatenate(normed, axis=1)], axis=0)
    act = silu_mul(dot_t(x, sg_ref[...]), dot_t(x, su_ref[...]))
    shared = dot(act, sd_ref[...])
    shared_ref[...] = shared[:col_n].astype(BF)
    mine = jnp.where(iota((dec_n, 1), 0) == (b >> 1), 1.0, 0.0) * jnp.where((b & 1) == 0, 1.0, 0.0)
    dec = [mine * shared[col_n:, j * slice_w : (j + 1) * slice_w] for j in range(fold)]

    n_dst, n_row, _ = out_ref.shape
    half = (n_row - 16) // 2
    for k in range(gate_ref.shape[0]):
        span = pl.ds(k * half, half)
        gate, up = 0.0, 0.0
        for s in range(n_dst):
            x = jnp.concatenate([rows_ref[s, span, :], normed[s]], axis=0)
            lanes = slice(s * slice_w, (s + 1) * slice_w)
            gate = gate + dot_t(x, gate_ref[k, :, lanes])
            up = up + dot_t(x, up_ref[k, :, lanes])
        act = silu_mul(gate, up)
        for d in range(n_dst):
            out = dot(act, down_ref[k, :, d * slice_w : (d + 1) * slice_w])
            out_ref[d, span, :] = out[:half].astype(BF)
            dec[d] = dec[d] + decw_ref[:, k : k + 1] * out[half:]

    line = iota((n_line, n_line), 0)
    col = iota((n_line, n_line), 1)
    swap = bits(col == (line & 7) * dec_n + (line >> 3))
    turned = dot(swap, jnp.concatenate([d.astype(BF) for d in dec], axis=0)).astype(BF)
    out_ref[:, n_row - 16 :, :] = turned.reshape(n_dst, 16, slice_w)
    hid_ref[...] = dot(swap, hidden).astype(BF).reshape(hid_ref.shape)


def return_kernel(got_ref, send_ref):
    n_src, n_all, slice_w = got_ref.shape
    n_dst = send_ref.shape[0]
    n_slot = n_all - 16
    half = n_slot // 2
    total = got_ref[0].astype(F32)
    for s in range(1, n_src):
        total = total + got_ref[s].astype(F32)
    total = total.astype(BF)
    column, place, second, slot = slot_of(iota((n_dst * 16, n_slot), 0))
    source = second * half + column * CAP + slot
    keep = jnp.logical_and(iota((n_dst * 16, n_slot), 1) == source, place < 2 * CAP)
    send_ref[:, :16, :] = dot(bits(keep), total[:n_slot]).astype(BF).reshape(n_dst, 16, slice_w)
    dec = total[n_slot:]
    for d in range(n_dst):
        send_ref[d, 16:, :] = dec


def combine_kernel(got_ref, comb_ref, shared_ref, hid_ref, send_ref, dec_ref):
    r = lax.axis_index("req")
    n_src, _, slice_w = got_ref.shape
    n_dst, pre_n, _ = send_ref.shape
    col_n = n_dst * pre_n
    slots = got_ref[:, :16, :].reshape(n_src * 16, slice_w)
    total = lax.dot_general(comb_ref[...], slots, (((0,), (0,)), ((), ())), preferred_element_type=F32)
    total = total[:col_n]
    first = rounded(total)
    shared = shared_ref[...].astype(F32)
    for d in range(n_dst):
        rows = slice(d * pre_n, (d + 1) * pre_n)
        send_ref[d] = jnp.concatenate(
            [first[rows], total[rows] - first[rows], shared[rows]], axis=1
        ).astype(BF)
    dec = hid_ref[r].astype(F32)
    moe = got_ref[0, 16:, :].astype(F32)
    for s in range(1, n_src):
        moe = moe + got_ref[s, 16:, :].astype(F32)
    dec = dec + moe
    dec_ref[...] = jnp.concatenate(
        [
            jnp.concatenate([dec[8 * i + j : 8 * i + j + 1] for j in range(8)], axis=1)
            for i in range(2)
        ],
        axis=0,
    ).astype(BF)


def finish_kernel(got_ref, res_ref, out_ref):
    n_src = got_ref.shape[0]
    slice_w = out_ref.shape[1] // n_src
    got = [got_ref[s].astype(F32) for s in range(n_src)]
    total = jnp.concatenate([g[:, :slice_w] + g[:, slice_w : 2 * slice_w] for g in got], axis=1)
    for g in got:
        total = total + g[:, 2 * slice_w :]
    out_ref[...] = (res_ref[...].astype(F32) + total).astype(BF)


def call(kernel, outs, args, flops, moved, specs=None, scratch=()):
    return pl.pallas_call(
        kernel,
        out_shape=outs,
        in_specs=specs or [VMEM] * len(args),
        out_specs=jax.tree.map(lambda _: VMEM, outs),
        scratch_shapes=scratch,
        cost_estimate=pl.CostEstimate(flops=flops, bytes_accessed=moved, transcendentals=0),
        compiler_params=pltpu.CompilerParams(vmem_limit_bytes=16 << 20),
    )(*args)


def local(
    prefill_resid,
    prefill_routes,
    prefill_scores,
    decode_resid,
    queries,
    latent_cache,
    new_latent,
    cache_lengths,
    decode_routes,
    decode_scores,
    norm_gain,
    absorb_key,
    absorb_value,
    out_proj,
    expert_gate,
    expert_up,
    expert_down,
    shared_gate,
    shared_up,
    shared_down,
):
    req_n = lax.axis_size("req")
    blk_n = lax.axis_size("blk")
    pre_n, width = prefill_resid.shape
    slice_w = width // req_n
    col_n = pre_n * req_n
    part_w = absorb_key.shape[2] + 128
    n_slot = 2 * CAP * blk_n
    gain = norm_gain[None]

    def shape(*dims, dtype=BF):
        return jax.ShapeDtypeStruct(dims, dtype)

    with jax.named_scope("start"):
        sources = (
            queries,
            absorb_key,
            prefill_resid,
            gain,
            prefill_routes,
            prefill_scores,
            decode_routes,
            decode_scores,
            new_latent,
            cache_lengths,
            jnp.swapaxes(latent_cache, 1, 2),
        )
        held = [pltpu.VMEM(a.shape, a.dtype) for a in sources]
        held[9] = pltpu.SMEM(cache_lengths.shape, cache_lengths.dtype)
        sent = call(
            start_kernel,
            shape(req_n, pre_n, width + 128 + part_w),
            tuple(pltpu.with_memory_space_constraint(a, pltpu.HBM) for a in sources),
            10**8,
            4 * 10**6,
            specs=[pl.BlockSpec(memory_space=pltpu.HBM)] * len(sources),
            scratch=held + [pltpu.SemaphoreType.DMA((len(sources),))],
        )
        got = exchange(sent, "req")
    with jax.named_scope("route"):
        sent, cols, comb, decw = call(
            route_kernel,
            (
                shape(blk_n, 16, slice_w),
                shape(col_n, width),
                shape(blk_n * 16, 128),
                shape(16, 128, dtype=F32),
            ),
            (got,),
            10**7,
            10**6,
        )
        got = exchange(sent, "blk")
    with jax.named_scope("heads"):
        sent = call(
            head_kernel,
            shape(req_n, n_slot + 8, slice_w),
            (got, absorb_value, out_proj, decode_resid),
            10**8,
            3 * 10**6,
        )
        rows = exchange(sent, "req")
    with jax.named_scope("hidden"):
        sent = call(sum_kernel, shape(blk_n, 8, slice_w), (rows,), 10**5, 3 * 10**5)
        got = exchange(sent, "blk")
    with jax.named_scope("experts"):
        sent, shared, hidden = call(
            terms_kernel,
            (
                shape(req_n, n_slot + 16, slice_w),
                shape(col_n, width),
                shape(req_n, 16, slice_w),
            ),
            (
                got,
                rows,
                cols,
                gain,
                decw,
                jnp.swapaxes(expert_gate, 1, 2),
                jnp.swapaxes(expert_up, 1, 2),
                expert_down,
                shared_gate.T,
                shared_up.T,
                shared_down,
            ),
            8 * 10**9,
            12 * 10**6,
        )
        got = exchange(sent, "req")
    with jax.named_scope("return"):
        sent = call(return_kernel, shape(blk_n, 32, slice_w), (got,), 10**8, 3 * 10**6)
        got = exchange(sent, "blk")
    with jax.named_scope("combine"):
        sent, decode_out = call(
            combine_kernel,
            (shape(req_n, pre_n, 2 * slice_w + width), shape(2, width)),
            (got, comb, shared, hidden),
            10**7,
            10**6,
        )
        got = exchange(sent, "req")
    with jax.named_scope("finish"):
        prefill_out = call(finish_kernel, shape(pre_n, width), (got, prefill_resid), 10**5, 10**5)
    return (prefill_out, decode_out)


def solution(mesh):
    return jax.shard_map(
        local,
        mesh=mesh,
        in_specs=(
            P(("blk", "req"), None),
            P(("blk", "req"), None),
            P(("blk", "req"), None),
            P("req", None),
            P("req", None, None),
            P("req", "blk", None),
            P("req", None),
            P("req"),
            P("req", None),
            P("req", None),
            P(),
            P(),
            P("req", None, None),
            P("req", None, None),
            P("blk", None, "req"),
            P("blk", None, "req"),
            P("blk", "req", None),
            P(None, "req"),
            P(None, "req"),
            P("req", None),
        ),
        out_specs=(P(("blk", "req"), None), P("req", None)),
        check_vma=False,
    )
```

```python
import jax
import jax.numpy as jnp
from jax import lax
from jax.experimental import pallas as pl
from jax.experimental.pallas import tpu as pltpu
from jax.sharding import PartitionSpec as P

NEG = -1e30
ROUTE_SCALE = 2.446
CAP = 6
BF = jnp.bfloat16
F32 = jnp.float32
I32 = jnp.int32
VMEM = pl.BlockSpec(memory_space=pltpu.VMEM)
SMEM = pl.BlockSpec(memory_space=pltpu.SMEM)


def exchange(payload, axis):
    return lax.all_to_all(payload, axis, 0, 0, tiled=True)


def dot(a, b):
    return jnp.dot(a, b, preferred_element_type=F32)


def dot_t(a, b):
    return lax.dot_general(a, b, (((1,), (1,)), ((), ())), preferred_element_type=F32)


def iota(shape, dim):
    return lax.broadcasted_iota(I32, shape, dim)


def bits(mask):
    return jnp.where(mask, 1.0, 0.0).astype(BF)


def rounded(values):
    return values.astype(BF).astype(F32)


def pieces(values):
    first = rounded(values)
    second = rounded(values - first)
    return [first, second, values - first - second]


def silu_mul(gate, up):
    return (gate * jax.nn.sigmoid(gate) * up).astype(BF)


def slot_of(row):
    place = row & 15
    second = (place >= CAP).astype(I32)
    return row >> 4, place, second, place - CAP * second


def start_kernel(*refs):
    count = (len(refs) - 2) // 2
    sources, out_ref, held, sems = refs[:count], refs[count], refs[count + 1 : -1], refs[-1]
    copies = [pltpu.make_async_copy(s, h, sems.at[n]) for n, (s, h) in enumerate(zip(sources, held))]
    for copy in copies:
        copy.start()
    q_ref, key_ref, res_ref, gain_ref, prt_ref, psc_ref, drt_ref, dsc_ref, new_ref, len_ref, cache_ref = held
    b = lax.axis_index("blk")
    for copy in copies[2:8]:
        copy.wait()
    pre_n, width = res_ref.shape
    n_req, heads, qw = q_ref.shape
    _, nope, latent = key_ref.shape
    positions = cache_ref.shape[2]
    scale = qw ** (-0.5)

    x = res_ref[...].astype(F32)
    mean_square = jnp.mean(x * x, axis=1, keepdims=True)
    rows = x * lax.rsqrt(mean_square + 1e-06) * gain_ref[...]

    def shares(sc):
        return rounded(sc / jnp.sum(sc, axis=1, keepdims=True) * ROUTE_SCALE)

    lane = iota((pre_n, 128), 1)
    row = iota((pre_n, 128), 0)
    top = prt_ref.shape[1]
    pr, ps = prt_ref[...].astype(F32), shares(psc_ref[...])
    dr, ds = drt_ref[...].astype(F32), shares(dsc_ref[...])
    meta = jnp.zeros((pre_n, 128), F32)
    for k in range(top):
        meta = jnp.where(lane == k, pr[:, k : k + 1], meta)
        meta = jnp.where(lane == top + k, ps[:, k : k + 1], meta)
        for i in range(n_req):
            at = jnp.logical_and(row == 2 * i, lane == 16 + k)
            meta = jnp.where(at, dr[i : i + 1, k : k + 1], meta)
            at = jnp.logical_and(row == 2 * i, lane == 16 + top + k)
            meta = jnp.where(at, ds[i : i + 1, k : k + 1], meta)

    for copy in copies[:2]:
        copy.wait()
    q_all = jnp.concatenate([q_ref[i] for i in range(n_req)], axis=0)
    q_nope = q_all[:, :nope]
    q_rope = q_all[:, nope:]
    q_head = iota((n_req * heads, latent), 0) & (heads - 1)
    q_lat = jnp.zeros((n_req * heads, latent), F32)
    for h in range(heads):
        q_lat = jnp.where(q_head == h, dot(q_nope, key_ref[h]), q_lat)
    q_lat = q_lat.astype(BF)

    for copy in copies[8:]:
        copy.wait()
    fresh_rows = new_ref[...].astype(F32)
    first = b == 0
    parts = []
    for i in range(n_req):
        ql = q_lat[i * heads : (i + 1) * heads]
        qr = q_rope[i * heads : (i + 1) * heads]
        s = (dot(ql, cache_ref[i, :latent, :]) + dot(qr, cache_ref[i, latent:, :])) * scale
        live = b * positions + iota((heads, positions), 1) < len_ref[i]
        s = jnp.where(live, s, NEG)
        new = fresh_rows[i : i + 1]
        fresh = jnp.sum(ql.astype(F32) * new[:, :latent], axis=1, keepdims=True)
        fresh = (fresh + jnp.sum(qr.astype(F32) * new[:, latent:], axis=1, keepdims=True)) * scale
        fresh = jnp.where(first, fresh, NEG)
        peak = jnp.maximum(jnp.max(s, axis=1, keepdims=True), fresh)
        expo = jnp.where(live, jnp.exp(s - peak), 0.0)
        fresh_w = jnp.where(first, jnp.exp(fresh - peak), 0.0)
        total = jnp.sum(expo, axis=1, keepdims=True) + fresh_w
        summed = dot_t(expo.astype(BF), cache_ref[i, :latent, :]) + rounded(fresh_w) * new[:, :latent]
        mean = summed / jnp.where(total > 0.0, total, 1.0)
        lane_h = iota((heads, 128), 1)
        stats = jnp.zeros((heads, 128), F32)
        for k, piece in enumerate(pieces(peak) + pieces(total)):
            stats = jnp.where(lane_h == k, piece, stats)
        parts.append(jnp.concatenate([mean, stats], axis=1))

    own = heads // out_ref.shape[0]
    for d in range(out_ref.shape[0]):
        att = jnp.concatenate([p[own * d : own * (d + 1)] for p in parts], axis=0)
        out_ref[d] = jnp.concatenate([rows, meta, att], axis=1).astype(BF)


def route_kernel(got_ref, send_ref, cols_ref, comb_ref, decw_ref):
    r = lax.axis_index("req")
    b = lax.axis_index("blk")
    n_src, pre_n, _ = got_ref.shape
    col_n, width = cols_ref.shape
    slice_w = send_ref.shape[2]
    blk_n = send_ref.shape[0]
    experts = 2 * blk_n
    top = 6
    full = jnp.concatenate([got_ref[s].astype(F32) for s in range(n_src)], axis=0)
    cols_ref[...] = full[:, :width].astype(BF)
    meta = full[:, width : width + 128]
    pairs = full[:, width + 128 :]

    expert = iota((col_n, experts), 1).astype(F32)
    named = jnp.zeros((col_n, experts), F32)
    weight = jnp.zeros((col_n, experts), F32)
    for k in range(top):
        hit = meta[:, k : k + 1] == expert
        named = jnp.where(hit, 1.0, named)
        weight = jnp.where(hit, meta[:, top + k : top + k + 1], weight)
    earlier = bits(iota((col_n, col_n), 1) < iota((col_n, col_n), 0))
    rank = dot(earlier, named.astype(BF))
    value = jnp.where(named > 0.0, rank + 1.0, 0.0)

    n_row = blk_n * 16
    column, place, second, slot = slot_of(iota((n_row, experts), 0))
    picks = jnp.logical_and(iota((n_row, experts), 1) == 2 * column + second, place < 2 * CAP)
    picks = bits(picks)
    rest = jnp.zeros((128 - col_n, experts), F32)
    value = dot_t(picks, jnp.concatenate([value, rest], axis=0).astype(BF))
    weight = dot_t(picks, jnp.concatenate([weight, rest], axis=0).astype(BF))
    row = iota((n_row, 128), 0)
    lane = iota((n_row, 128), 1)
    _, _, _, slot = slot_of(row)
    chosen = value == (slot + 1).astype(F32)
    comb_ref[...] = jnp.where(chosen, weight, 0.0).astype(BF)
    carried = jnp.logical_and(lane >= col_n, row == (lane & (col_n - 1)) * 16 + 11 + (lane >> 5))
    mine = cols_ref[:, pl.ds(pl.multiple_of(r * slice_w, slice_w), slice_w)]
    last = jnp.concatenate([pairs[:, 2 * slice_w :], jnp.zeros((col_n, slice_w - 128), F32)], axis=1)
    data = jnp.concatenate(
        [mine, pairs[:, :slice_w].astype(BF), pairs[:, slice_w : 2 * slice_w].astype(BF), last.astype(BF)],
        axis=0,
    )
    moved = dot(bits(jnp.logical_or(chosen, carried)), data).astype(BF)
    send_ref[...] = moved.reshape(send_ref.shape)

    lane = iota((col_n, 128), 1)
    dec = jnp.zeros((col_n, 128), F32)
    for k in range(2):
        own = (2 * b + k).astype(F32)
        got = jnp.zeros((col_n, 1), F32)
        for j in range(top):
            hit = meta[:, 16 + j : 17 + j] == own
            got = jnp.where(hit, meta[:, 16 + top + j : 17 + top + j], got)
        dec = jnp.where(lane == k, got, dec)
    even = bits(iota((col_n // 2, col_n), 1) == 2 * iota((col_n // 2, col_n), 0))
    decw_ref[...] = dot(even, dec.astype(BF))


def head_kernel(got_ref, val_ref, proj_ref, res_ref, send_ref):
    r = lax.axis_index("req")
    b = lax.axis_index("blk")
    n_src, block, slice_w = got_ref.shape
    n_dst, n_out, _ = send_ref.shape
    n_slot = n_out - 8
    half = n_slot // 2
    got = got_ref[...].reshape(n_src * block, slice_w)
    column, place, second, slot = slot_of(iota((n_slot, n_src * block), 1))
    target = second * half + column * CAP + slot
    keep = jnp.logical_and(iota((n_slot, n_src * block), 0) == target, place < 2 * CAP)
    slots = dot(bits(keep), got).astype(BF)
    for d in range(n_dst):
        send_ref[d, :n_slot, :] = slots

    line = iota((3 * n_src, n_src * block), 0)
    part = iota((3 * n_src, n_src * block), 1) == (line & (n_src - 1)) * block + 12 + (line >> 5)
    part = dot(bits(part), got)
    stats = part[2 * n_src :]
    peak = stats[:, 0:1] + stats[:, 1:2] + stats[:, 2:3]
    total = stats[:, 3:4] + stats[:, 4:5] + stats[:, 5:6]
    share = total * jnp.exp(peak - jnp.max(peak, axis=0, keepdims=True))
    whole = jnp.sum(share, axis=0, keepdims=True)
    low = jnp.sum(part[:n_src] * share, axis=0, keepdims=True) / whole
    high = jnp.sum(part[n_src : 2 * n_src] * share, axis=0, keepdims=True) / whole
    o_latent = jnp.broadcast_to(jnp.concatenate([low, high], axis=1), (8, 2 * slice_w)).astype(BF)
    head = b & 1
    request = b >> 1
    head_value = dot(o_latent, val_ref[head]).astype(BF)
    projected = dot(head_value, proj_ref[head])[0:1]
    resid = res_ref[...].astype(F32)
    resid = jnp.where(iota(resid.shape, 0) == (request & 1), resid, 0.0)
    resid = jnp.sum(resid, axis=0, keepdims=True)
    owner = jnp.logical_and(request >> 1 == r, head == 0)
    projected = projected + jnp.where(owner, resid, 0.0)
    folded = jnp.concatenate(
        [projected[:, slice_w * j : slice_w * (j + 1)] for j in range(8)], axis=0
    ).astype(BF)
    for d in range(n_dst):
        send_ref[d, n_slot:, :] = folded


def sum_kernel(got_ref, send_ref):
    n_src, n_all, _ = got_ref.shape
    total = got_ref[0, n_all - 8 :, :].astype(F32)
    for s in range(1, n_src):
        total = total + got_ref[s, n_all - 8 :, :].astype(F32)
    total = total.astype(BF)
    for d in range(send_ref.shape[0]):
        send_ref[d] = total


def terms_kernel(
    got_ref,
    rows_ref,
    cols_ref,
    gain_ref,
    decw_ref,
    gate_ref,
    up_ref,
    down_ref,
    sg_ref,
    su_ref,
    sd_ref,
    out_ref,
    shared_ref,
    hid_ref,
):
    b = lax.axis_index("blk")
    n_src, fold, slice_w = got_ref.shape
    dec_n = n_src // 2
    n_line = fold * dec_n
    got = got_ref[...].reshape(n_src * fold, slice_w)
    line = iota((n_line, n_src * fold), 0)
    col = iota((n_line, n_src * fold), 1)
    pick = jnp.logical_and(col >> 4 == (line & (dec_n - 1)), (col & 7) == line >> 4)
    hidden = dot(bits(pick), got).astype(BF)
    wide = hidden.astype(F32)
    chunks = [wide[j * dec_n : (j + 1) * dec_n] for j in range(fold)]
    square = sum(jnp.sum(c * c, axis=1, keepdims=True) for c in chunks)
    factor = lax.rsqrt(square / (fold * slice_w) + 1e-06)
    normed = [
        (c * factor * gain_ref[:, j * slice_w : (j + 1) * slice_w]).astype(BF)
        for j, c in enumerate(chunks)
    ]

    col_n = cols_ref.shape[0]
    x = jnp.concatenate([cols_ref[...], jnp.concatenate(normed, axis=1)], axis=0)
    act = silu_mul(dot_t(x, sg_ref[...]), dot_t(x, su_ref[...]))
    shared = dot(act, sd_ref[...])
    shared_ref[...] = shared[:col_n].astype(BF)
    mine = jnp.where(iota((dec_n, 1), 0) == (b >> 1), 1.0, 0.0) * jnp.where((b & 1) == 0, 1.0, 0.0)
    dec = [mine * shared[col_n:, j * slice_w : (j + 1) * slice_w] for j in range(fold)]

    n_dst, n_row, _ = out_ref.shape
    half = (n_row - 16) // 2
    for k in range(gate_ref.shape[0]):
        span = pl.ds(k * half, half)
        gate, up = 0.0, 0.0
        for s in range(n_dst):
            x = jnp.concatenate([rows_ref[s, span, :], normed[s]], axis=0)
            lanes = slice(s * slice_w, (s + 1) * slice_w)
            gate = gate + dot_t(x, gate_ref[k, :, lanes])
            up = up + dot_t(x, up_ref[k, :, lanes])
        act = silu_mul(gate, up)
        for d in range(n_dst):
            out = dot(act, down_ref[k, :, d * slice_w : (d + 1) * slice_w])
            out_ref[d, span, :] = out[:half].astype(BF)
            dec[d] = dec[d] + decw_ref[:, k : k + 1] * out[half:]

    line = iota((n_line, n_line), 0)
    col = iota((n_line, n_line), 1)
    swap = bits(col == (line & 7) * dec_n + (line >> 3))
    turned = dot(swap, jnp.concatenate([d.astype(BF) for d in dec], axis=0)).astype(BF)
    out_ref[:, n_row - 16 :, :] = turned.reshape(n_dst, 16, slice_w)
    hid_ref[...] = dot(swap, hidden).reshape(hid_ref.shape).astype(BF)


def hidden_sum_kernel(got_ref, slots_ref, keep_ref, give_ref):
    b = lax.axis_index("blk")
    n_src = got_ref.shape[0]
    n_slot = slots_ref.shape[0]
    total = got_ref[0].astype(F32)
    for s in range(1, n_src):
        total = total + got_ref[s].astype(F32)
    slots_ref[...] = total[:n_slot].astype(BF)
    dec = total[n_slot:]
    low = jnp.concatenate([dec[0:4], dec[8:12]], axis=0)
    high = jnp.concatenate([dec[4:8], dec[12:16]], axis=0)
    even = (b & 1) == 0
    keep_ref[...] = jnp.where(even, low, high)
    give_ref[...] = jnp.where(even, high, low).astype(BF)


def return_kernel(slots_ref, keep_ref, other_ref, send_ref):
    n_slot = slots_ref.shape[0]
    n_dst, block, _ = send_ref.shape
    half = n_slot // 2
    dec = (keep_ref[...] + other_ref[...].astype(F32)).astype(BF)
    data = jnp.concatenate([slots_ref[...], dec, jnp.zeros_like(dec)], axis=0)
    column, place, second, slot = slot_of(iota((n_dst * block, n_slot + 16), 0))
    col = iota((n_dst * block, n_slot + 16), 1)
    source = jnp.where(
        place < 2 * CAP,
        second * half + column * CAP + slot,
        n_slot + 4 * (column & 1) + place - 2 * CAP,
    )
    send_ref[...] = dot(bits(col == source), data).astype(BF).reshape(send_ref.shape)


def combine_kernel(got_ref, comb_ref, shared_ref, hid_ref, send_ref, dec_ref):
    r = lax.axis_index("req")
    b = lax.axis_index("blk")
    n_src, _, slice_w = got_ref.shape
    n_dst, pre_n, _ = send_ref.shape
    col_n = n_dst * pre_n
    slots = got_ref[...].reshape(n_src * 16, slice_w)
    total = lax.dot_general(comb_ref[...], slots, (((0,), (0,)), ((), ())), preferred_element_type=F32)
    total = total[:col_n]
    first = rounded(total)
    shared = shared_ref[...].astype(F32)
    for d in range(n_dst):
        rows = slice(d * pre_n, (d + 1) * pre_n)
        send_ref[d] = jnp.concatenate(
            [first[rows], total[rows] - first[rows], shared[rows]], axis=1
        ).astype(BF)
    line = iota((8, n_src * 16), 0)
    col = iota((8, n_src * 16), 1)
    pick = jnp.logical_and((col & 15) == 12 + (line & 3), ((col >> 4) & 1) == line >> 2)
    moe = dot(bits(pick), slots)
    dec_ref[...] = (hid_ref[2 * r + (b & 1)].astype(F32) + moe).astype(BF)


def finish_kernel(got_ref, res_ref, own_ref, other_ref, out_ref, dec_ref):
    b = lax.axis_index("blk")
    n_src = got_ref.shape[0]
    slice_w = out_ref.shape[1] // n_src
    got = [got_ref[s].astype(F32) for s in range(n_src)]
    total = jnp.concatenate([g[:, :slice_w] + g[:, slice_w : 2 * slice_w] for g in got], axis=1)
    for g in got:
        total = total + g[:, 2 * slice_w :]
    out_ref[...] = (res_ref[...].astype(F32) + total).astype(BF)

    def flat(ref):
        folded = ref[...].astype(F32)
        return jnp.concatenate([folded[j : j + 1] for j in range(n_src)], axis=1)

    own, other = flat(own_ref), flat(other_ref)
    even = (b & 1) == 0
    dec_ref[...] = jnp.concatenate(
        [jnp.where(even, own, other), jnp.where(even, other, own)], axis=0
    ).astype(BF)


def call(kernel, outs, args, flops, moved, specs=None, scratch=()):
    return pl.pallas_call(
        kernel,
        out_shape=outs,
        in_specs=specs or [VMEM] * len(args),
        out_specs=jax.tree.map(lambda _: VMEM, outs),
        scratch_shapes=scratch,
        cost_estimate=pl.CostEstimate(flops=flops, bytes_accessed=moved, transcendentals=0),
        compiler_params=pltpu.CompilerParams(vmem_limit_bytes=16 << 20),
    )(*args)


def local(
    prefill_resid,
    prefill_routes,
    prefill_scores,
    decode_resid,
    queries,
    latent_cache,
    new_latent,
    cache_lengths,
    decode_routes,
    decode_scores,
    norm_gain,
    absorb_key,
    absorb_value,
    out_proj,
    expert_gate,
    expert_up,
    expert_down,
    shared_gate,
    shared_up,
    shared_down,
):
    req_n = lax.axis_size("req")
    blk_n = lax.axis_size("blk")
    pre_n, width = prefill_resid.shape
    slice_w = width // req_n
    col_n = pre_n * req_n
    part_w = absorb_key.shape[2] + 128
    n_slot = 2 * CAP * blk_n
    gain = norm_gain[None]
    sibling = [(i, i ^ 1) for i in range(blk_n)]

    def shape(*dims, dtype=BF):
        return jax.ShapeDtypeStruct(dims, dtype)

    with jax.named_scope("start"):
        sources = (
            queries,
            absorb_key,
            prefill_resid,
            gain,
            prefill_routes,
            prefill_scores,
            decode_routes,
            decode_scores,
            new_latent,
            cache_lengths,
            jnp.swapaxes(latent_cache, 1, 2),
        )
        held = [pltpu.VMEM(a.shape, a.dtype) for a in sources]
        held[9] = pltpu.SMEM(cache_lengths.shape, cache_lengths.dtype)
        sent = call(
            start_kernel,
            shape(req_n, pre_n, width + 128 + part_w),
            tuple(pltpu.with_memory_space_constraint(a, pltpu.HBM) for a in sources),
            10**8,
            4 * 10**6,
            specs=[pl.BlockSpec(memory_space=pltpu.HBM)] * len(sources),
            scratch=held + [pltpu.SemaphoreType.DMA((len(sources),))],
        )
        got = exchange(sent, "req")
    with jax.named_scope("route"):
        sent, cols, comb, decw = call(
            route_kernel,
            (
                shape(blk_n, 16, slice_w),
                shape(col_n, width),
                shape(blk_n * 16, 128),
                shape(16, 128, dtype=F32),
            ),
            (got,),
            10**7,
            10**6,
        )
        got = exchange(sent, "blk")
    with jax.named_scope("heads"):
        sent = call(
            head_kernel,
            shape(req_n, n_slot + 8, slice_w),
            (got, absorb_value, out_proj, decode_resid),
            10**8,
            3 * 10**6,
        )
        rows = exchange(sent, "req")
    with jax.named_scope("hidden"):
        sent = call(sum_kernel, shape(blk_n, 8, slice_w), (rows,), 10**5, 3 * 10**5)
        got = exchange(sent, "blk")
    with jax.named_scope("experts"):
        sent, shared, hidden = call(
            terms_kernel,
            (
                shape(req_n, n_slot + 16, slice_w),
                shape(col_n, width),
                shape(2 * req_n, 8, slice_w),
            ),
            (
                got,
                rows,
                cols,
                gain,
                decw,
                jnp.swapaxes(expert_gate, 1, 2),
                jnp.swapaxes(expert_up, 1, 2),
                expert_down,
                shared_gate.T,
                shared_up.T,
                shared_down,
            ),
            8 * 10**9,
            12 * 10**6,
        )
        got = exchange(sent, "req")
    with jax.named_scope("return"):
        slots, keep, give = call(
            hidden_sum_kernel,
            (shape(n_slot, slice_w), shape(8, slice_w, dtype=F32), shape(8, slice_w)),
            (got,),
            10**6,
            2 * 10**6,
        )
        other = lax.ppermute(give, "blk", sibling)
        sent = call(return_kernel, shape(blk_n, 16, slice_w), (slots, keep, other), 10**8, 10**6)
        got = exchange(sent, "blk")
    with jax.named_scope("combine"):
        sent, own_row = call(
            combine_kernel,
            (shape(req_n, pre_n, 2 * slice_w + width), shape(8, slice_w)),
            (got, comb, shared, hidden),
            10**7,
            10**6,
        )
        other_row = lax.ppermute(own_row, "blk", sibling)
        got = exchange(sent, "req")
    with jax.named_scope("finish"):
        prefill_out, decode_out = call(
            finish_kernel,
            (shape(pre_n, width), shape(2, width)),
            (got, prefill_resid, own_row, other_row),
            10**5,
            10**5,
        )
    return (prefill_out, decode_out)


def solution(mesh):
    return jax.shard_map(
        local,
        mesh=mesh,
        in_specs=(
            P(("blk", "req"), None),
            P(("blk", "req"), None),
            P(("blk", "req"), None),
            P("req", None),
            P("req", None, None),
            P("req", "blk", None),
            P("req", None),
            P("req"),
            P("req", None),
            P("req", None),
            P(),
            P(),
            P("req", None, None),
            P("req", None, None),
            P("blk", None, "req"),
            P("blk", None, "req"),
            P("blk", "req", None),
            P(None, "req"),
            P(None, "req"),
            P("req", None),
        ),
        out_specs=(P(("blk", "req"), None), P("req", None)),
        check_vma=False,
    )
```

```python
import jax
import jax.numpy as jnp
from jax import lax
from jax.experimental import pallas as pl
from jax.experimental.pallas import tpu as pltpu
from jax.sharding import PartitionSpec as P

NEG = -1e30
ROUTE_SCALE = 2.446
CAP = 6
HEAD = 16
SLACK = 48
BF = jnp.bfloat16
F32 = jnp.float32
I32 = jnp.int32
VMEM = pl.BlockSpec(memory_space=pltpu.VMEM)
SMEM = pl.BlockSpec(memory_space=pltpu.SMEM)


def exchange(payload, axis):
    return lax.all_to_all(payload, axis, 0, 0, tiled=True)


def dot(a, b):
    return jnp.dot(a, b, preferred_element_type=F32)


def dot_t(a, b):
    return lax.dot_general(a, b, (((1,), (1,)), ((), ())), preferred_element_type=F32)


def iota(shape, dim):
    return lax.broadcasted_iota(I32, shape, dim)


def bits(mask):
    return jnp.where(mask, 1.0, 0.0).astype(BF)


def rounded(values):
    return values.astype(BF).astype(F32)


def pieces(values):
    first = rounded(values)
    second = rounded(values - first)
    return [first, second, values - first - second]


def silu_mul(gate, up):
    return (gate * jax.nn.sigmoid(gate) * up).astype(BF)


def slot_of(row):
    place = row & 15
    second = (place >= CAP).astype(I32)
    return row >> 4, place, second, place - CAP * second


def start_kernel(*refs):
    count = (len(refs) - 2) // 2
    sources, out_ref, held, sems = refs[:count], refs[count], refs[count + 1 : -1], refs[-1]
    copies = [pltpu.make_async_copy(s, h, sems.at[n]) for n, (s, h) in enumerate(zip(sources, held))]
    for copy in copies:
        copy.start()
    q_ref, key_ref, res_ref, gain_ref, prt_ref, psc_ref, drt_ref, dsc_ref, new_ref, len_ref, cache_ref = held
    b = lax.axis_index("blk")
    for copy in copies[2:8]:
        copy.wait()
    pre_n, width = res_ref.shape
    n_req, heads, qw = q_ref.shape
    _, nope, latent = key_ref.shape
    positions = cache_ref.shape[2]
    scale = qw ** (-0.5)

    x = res_ref[...].astype(F32)
    mean_square = jnp.mean(x * x, axis=1, keepdims=True)
    rows = x * lax.rsqrt(mean_square + 1e-06) * gain_ref[...]

    def shares(sc):
        return rounded(sc / jnp.sum(sc, axis=1, keepdims=True) * ROUTE_SCALE)

    lane = iota((pre_n, 128), 1)
    row = iota((pre_n, 128), 0)
    top = prt_ref.shape[1]
    pr, ps = prt_ref[...].astype(F32), shares(psc_ref[...])
    dr, ds = drt_ref[...].astype(F32), shares(dsc_ref[...])
    meta = jnp.zeros((pre_n, 128), F32)
    for k in range(top):
        meta = jnp.where(lane == k, pr[:, k : k + 1], meta)
        meta = jnp.where(lane == top + k, ps[:, k : k + 1], meta)
        for i in range(n_req):
            at = jnp.logical_and(row == 2 * i, lane == 16 + k)
            meta = jnp.where(at, dr[i : i + 1, k : k + 1], meta)
            at = jnp.logical_and(row == 2 * i, lane == 16 + top + k)
            meta = jnp.where(at, ds[i : i + 1, k : k + 1], meta)

    for copy in copies[:2]:
        copy.wait()
    q_all = jnp.concatenate([q_ref[i] for i in range(n_req)], axis=0)
    q_nope = q_all[:, :nope]
    q_rope = q_all[:, nope:]
    q_head = iota((n_req * heads, latent), 0) & (heads - 1)
    q_lat = jnp.zeros((n_req * heads, latent), F32)
    for h in range(heads):
        q_lat = jnp.where(q_head == h, dot(q_nope, key_ref[h]), q_lat)
    q_lat = q_lat.astype(BF)

    for copy in copies[8:]:
        copy.wait()
    fresh_rows = new_ref[...].astype(F32)
    first = b == 0
    parts = []
    for i in range(n_req):
        ql = q_lat[i * heads : (i + 1) * heads]
        qr = q_rope[i * heads : (i + 1) * heads]
        s = (dot(ql, cache_ref[i, :latent, :]) + dot(qr, cache_ref[i, latent:, :])) * scale
        live = b * positions + iota((heads, positions), 1) < len_ref[i]
        s = jnp.where(live, s, NEG)
        new = fresh_rows[i : i + 1]
        fresh = jnp.sum(ql.astype(F32) * new[:, :latent], axis=1, keepdims=True)
        fresh = (fresh + jnp.sum(qr.astype(F32) * new[:, latent:], axis=1, keepdims=True)) * scale
        fresh = jnp.where(first, fresh, NEG)
        peak = jnp.maximum(jnp.max(s, axis=1, keepdims=True), fresh)
        expo = jnp.where(live, jnp.exp(s - peak), 0.0)
        fresh_w = jnp.where(first, jnp.exp(fresh - peak), 0.0)
        total = jnp.sum(expo, axis=1, keepdims=True) + fresh_w
        summed = dot_t(expo.astype(BF), cache_ref[i, :latent, :]) + rounded(fresh_w) * new[:, :latent]
        mean = summed / jnp.where(total > 0.0, total, 1.0)
        lane_h = iota((heads, 128), 1)
        stats = jnp.zeros((heads, 128), F32)
        for k, piece in enumerate(pieces(peak) + pieces(total)):
            stats = jnp.where(lane_h == k, piece, stats)
        parts.append(jnp.concatenate([mean, stats], axis=1))

    own = heads // out_ref.shape[0]
    for d in range(out_ref.shape[0]):
        att = jnp.concatenate([p[own * d : own * (d + 1)] for p in parts], axis=0)
        out_ref[d] = jnp.concatenate([rows, meta, att], axis=1).astype(BF)


def route_kernel(got_ref, send_ref, cols_ref, comb_ref, decw_ref):
    r = lax.axis_index("req")
    b = lax.axis_index("blk")
    n_src, pre_n, _ = got_ref.shape
    col_n, width = cols_ref.shape
    slice_w = send_ref.shape[2]
    blk_n = send_ref.shape[0]
    experts = 2 * blk_n
    top = 6
    full = jnp.concatenate([got_ref[s].astype(F32) for s in range(n_src)], axis=0)
    cols_ref[...] = full[:, :width].astype(BF)
    meta = full[:, width : width + 128]
    pairs = full[:, width + 128 :]

    expert = iota((col_n, experts), 1).astype(F32)
    named = jnp.zeros((col_n, experts), F32)
    weight = jnp.zeros((col_n, experts), F32)
    for k in range(top):
        hit = meta[:, k : k + 1] == expert
        named = jnp.where(hit, 1.0, named)
        weight = jnp.where(hit, meta[:, top + k : top + k + 1], weight)
    earlier = bits(iota((col_n, col_n), 1) < iota((col_n, col_n), 0))
    rank = dot(earlier, named.astype(BF))
    value = jnp.where(named > 0.0, rank + 1.0, 0.0)

    n_row = blk_n * 16
    column, place, second, slot = slot_of(iota((n_row, experts), 0))
    picks = jnp.logical_and(iota((n_row, experts), 1) == 2 * column + second, place < 2 * CAP)
    picks = bits(picks)
    rest = jnp.zeros((128 - col_n, experts), F32)
    value = dot_t(picks, jnp.concatenate([value, rest], axis=0).astype(BF))
    weight = dot_t(picks, jnp.concatenate([weight, rest], axis=0).astype(BF))
    row = iota((n_row, 128), 0)
    lane = iota((n_row, 128), 1)
    _, _, _, slot = slot_of(row)
    chosen = value == (slot + 1).astype(F32)
    comb_ref[...] = jnp.where(chosen, weight, 0.0).astype(BF)
    carried = jnp.logical_and(lane >= col_n, row == (lane & (col_n - 1)) * 16 + 11 + (lane >> 5))
    mine = cols_ref[:, pl.ds(pl.multiple_of(r * slice_w, slice_w), slice_w)]
    line = iota((col_n, experts), 0)
    lane = iota((col_n, experts), 1)
    tail = jnp.zeros((col_n, slice_w - 128), F32)
    for k in range(2):
        count = dot_t(bits(lane == 2 * line + k), named.astype(BF))
        count = jnp.sum(count, axis=1, keepdims=True)
        tail = jnp.where(iota(tail.shape, 1) == k, count, tail)
    last = jnp.concatenate([pairs[:, 2 * slice_w :], tail], axis=1)
    data = jnp.concatenate(
        [mine, pairs[:, :slice_w].astype(BF), pairs[:, slice_w : 2 * slice_w].astype(BF), last.astype(BF)],
        axis=0,
    )
    moved = dot(bits(jnp.logical_or(chosen, carried)), data).astype(BF)
    send_ref[...] = moved.reshape(send_ref.shape)

    lane = iota((col_n, 128), 1)
    dec = jnp.zeros((col_n, 128), F32)
    for k in range(2):
        own = (2 * b + k).astype(F32)
        got = jnp.zeros((col_n, 1), F32)
        for j in range(top):
            hit = meta[:, 16 + j : 17 + j] == own
            got = jnp.where(hit, meta[:, 16 + top + j : 17 + top + j], got)
        dec = jnp.where(lane == k, got, dec)
    even = bits(iota((col_n // 2, col_n), 1) == 2 * iota((col_n // 2, col_n), 0))
    decw_ref[...] = dot(even, dec.astype(BF))


def head_kernel(got_ref, val_ref, proj_ref, res_ref, send_ref, keep_ref, info_ref):
    r = lax.axis_index("req")
    b = lax.axis_index("blk")
    n_src, block, slice_w = got_ref.shape
    n_dst, n_out, _ = send_ref.shape
    n_slot = n_out - HEAD
    n_col = n_src * block
    got = got_ref[...].reshape(n_col, slice_w)
    line = iota((3 * n_src, n_src * block), 0)
    part = iota((3 * n_src, n_src * block), 1) == (line & (n_src - 1)) * block + 12 + (line >> 5)
    part = dot(bits(part), got)
    stats = part[2 * n_src :]

    count = stats[:, 128:]
    earlier = bits(iota((n_src, n_src), 1) < iota((n_src, n_src), 0))
    before = dot(earlier, count.astype(BF))
    spread = bits(iota((n_src, n_col), 1) >> 4 == iota((n_src, n_col), 0))
    table = jnp.concatenate([before, count], axis=1).astype(BF)
    table = lax.dot_general(table, spread, (((0,), (0,)), ((), ())), preferred_element_type=F32)
    used = jnp.sum(count, axis=0, keepdims=True)
    first_n = used[:, 0:1]
    column, place, second, slot = slot_of(iota((1, n_col), 1))
    slot = slot.astype(F32)
    width = count.shape[1]
    target = jnp.where(second == 1, table[1:2] + first_n, table[0:1]) + slot
    named = jnp.where(second == 1, table[width + 1 : width + 2], table[width : width + 1])
    target = jnp.where(jnp.logical_and(slot < named, place < 2 * CAP), target, -1.0)
    keep = bits(iota((n_slot, n_col), 0).astype(F32) == target)
    keep_ref[...] = keep
    slots = dot(keep, got).astype(BF)
    for d in range(n_dst):
        send_ref[d, HEAD:, :] = slots
    both = first_n + used[:, 1:2]
    index = jnp.zeros((1, 1), F32)
    for size in bucket_sizes(n_slot)[:-1]:
        index = index + jnp.where(both > size, 1.0, 0.0)
    lane = iota(info_ref.shape, 1)
    info_ref[...] = jnp.where(lane == 0, index, jnp.where(lane == 1, first_n, 0.0)).astype(I32)

    peak = stats[:, 0:1] + stats[:, 1:2] + stats[:, 2:3]
    total = stats[:, 3:4] + stats[:, 4:5] + stats[:, 5:6]
    share = total * jnp.exp(peak - jnp.max(peak, axis=0, keepdims=True))
    whole = jnp.sum(share, axis=0, keepdims=True)
    low = jnp.sum(part[:n_src] * share, axis=0, keepdims=True) / whole
    high = jnp.sum(part[n_src : 2 * n_src] * share, axis=0, keepdims=True) / whole
    o_latent = jnp.broadcast_to(jnp.concatenate([low, high], axis=1), (8, 2 * slice_w)).astype(BF)
    head = b & 1
    request = b >> 1
    head_value = dot(o_latent, val_ref[head]).astype(BF)
    projected = dot(head_value, proj_ref[head])[0:1]
    resid = res_ref[...].astype(F32)
    resid = jnp.where(iota(resid.shape, 0) == (request & 1), resid, 0.0)
    resid = jnp.sum(resid, axis=0, keepdims=True)
    owner = jnp.logical_and(request >> 1 == r, head == 0)
    projected = projected + jnp.where(owner, resid, 0.0)
    folded = jnp.concatenate(
        [projected[:, slice_w * j : slice_w * (j + 1)] for j in range(8)], axis=0
    )
    folded = jnp.concatenate([folded, jnp.zeros((HEAD - 8, slice_w), F32)], axis=0).astype(BF)
    for d in range(n_dst):
        send_ref[d, :HEAD, :] = folded


def sum_kernel(got_ref, send_ref):
    n_src = got_ref.shape[0]
    total = got_ref[0, :HEAD, :].astype(F32)
    for s in range(1, n_src):
        total = total + got_ref[s, :HEAD, :].astype(F32)
    total = total[:8].astype(BF)
    for d in range(send_ref.shape[0]):
        send_ref[d] = total


def terms_kernel(
    got_ref,
    rows_ref,
    cols_ref,
    gain_ref,
    decw_ref,
    info_ref,
    gate_ref,
    up_hbm,
    down_hbm,
    sg_hbm,
    su_hbm,
    sd_hbm,
    out_ref,
    shared_ref,
    hid_ref,
    up_ref,
    down_ref,
    sg_ref,
    su_ref,
    sd_ref,
    sems,
):
    loads = []
    pairs = [(h.at[k], v.at[k]) for k in range(2) for h, v in ((up_hbm, up_ref), (down_hbm, down_ref))]
    for source, held in pairs + [(sg_hbm, sg_ref), (su_hbm, su_ref), (sd_hbm, sd_ref)]:
        loads.append(pltpu.make_async_copy(source, held, sems.at[len(loads)]))
        loads[-1].start()
    b = lax.axis_index("blk")
    n_src, fold, slice_w = got_ref.shape
    dec_n = n_src // 2
    n_line = fold * dec_n
    got = got_ref[...].reshape(n_src * fold, slice_w)
    line = iota((n_line, n_src * fold), 0)
    col = iota((n_line, n_src * fold), 1)
    pick = jnp.logical_and(col >> 4 == (line & (dec_n - 1)), (col & 7) == line >> 4)
    hidden = dot(bits(pick), got).astype(BF)
    wide = hidden.astype(F32)
    chunks = [wide[j * dec_n : (j + 1) * dec_n] for j in range(fold)]
    square = sum(jnp.sum(c * c, axis=1, keepdims=True) for c in chunks)
    factor = lax.rsqrt(square / (fold * slice_w) + 1e-06)
    normed = [
        (c * factor * gain_ref[:, j * slice_w : (j + 1) * slice_w]).astype(BF)
        for j, c in enumerate(chunks)
    ]

    n_dst, n_row, _ = out_ref.shape
    half = (n_row - HEAD - SLACK) // 2
    first_n = jnp.max(jnp.where(iota(info_ref.shape, 1) == 1, info_ref[...], 0).astype(F32)).astype(I32)
    start = pl.multiple_of(HEAD + ((first_n >> 4) << 4), 16)
    dec = [jnp.zeros((dec_n, slice_w), F32)] * fold
    for k in range(gate_ref.shape[0]):
        size = half if k == 0 else half + SLACK
        span = pl.ds(HEAD, size) if k == 0 else pl.ds(start, size)
        gate, up = 0.0, 0.0
        loads[2 * k].wait()
        for s in range(n_dst):
            x = jnp.concatenate([rows_ref[s, span, :], normed[s]], axis=0)
            lanes = slice(s * slice_w, (s + 1) * slice_w)
            gate = gate + dot_t(x, gate_ref[k, :, lanes])
            up = up + dot_t(x, up_ref[k, :, lanes])
        act = silu_mul(gate, up)
        loads[2 * k + 1].wait()
        later = iota((size, slice_w), 0) + (start - HEAD) >= first_n
        for d in range(n_dst):
            out = dot(act, down_ref[k, :, d * slice_w : (d + 1) * slice_w])
            dec[d] = dec[d] + decw_ref[:, k : k + 1] * out[size:]
            rows = out[:size]
            if k == 1:
                rows = jnp.where(later, rows, out_ref[d, span, :].astype(F32))
            out_ref[d, span, :] = rows.astype(BF)

    col_n = cols_ref.shape[0]
    for load in loads[4:]:
        load.wait()
    x = jnp.concatenate([cols_ref[...], jnp.concatenate(normed, axis=1)], axis=0)
    act = silu_mul(dot_t(x, sg_ref[...]), dot_t(x, su_ref[...]))
    shared = dot(act, sd_ref[...])
    shared_ref[...] = shared[:col_n].astype(BF)
    mine = jnp.where(iota((dec_n, 1), 0) == (b >> 1), 1.0, 0.0) * jnp.where((b & 1) == 0, 1.0, 0.0)
    dec = [dec[j] + mine * shared[col_n:, j * slice_w : (j + 1) * slice_w] for j in range(fold)]

    line = iota((n_line, n_line), 0)
    col = iota((n_line, n_line), 1)
    swap = bits(col == (line & 7) * dec_n + (line >> 3))
    turned = dot(swap, jnp.concatenate([d.astype(BF) for d in dec], axis=0)).astype(BF)
    out_ref[:, :HEAD, :] = turned.reshape(n_dst, 16, slice_w)
    hid_ref[...] = dot(swap, hidden).reshape(hid_ref.shape).astype(BF)


def hidden_sum_kernel(got_ref, slots_ref, keep_ref, give_ref):
    b = lax.axis_index("blk")
    n_src = got_ref.shape[0]
    total = got_ref[0].astype(F32)
    for s in range(1, n_src):
        total = total + got_ref[s].astype(F32)
    slots_ref[...] = total[HEAD:].astype(BF)
    dec = total[:HEAD]
    low = jnp.concatenate([dec[0:4], dec[8:12]], axis=0)
    high = jnp.concatenate([dec[4:8], dec[12:16]], axis=0)
    even = (b & 1) == 0
    keep_ref[...] = jnp.where(even, low, high)
    give_ref[...] = jnp.where(even, high, low).astype(BF)


def return_kernel(slots_ref, keep_ref, mine_ref, other_ref, send_ref):
    n_dst, block, _ = send_ref.shape
    dec = (mine_ref[...] + other_ref[...].astype(F32)).astype(BF)
    column, place, second, slot = slot_of(iota((n_dst * block, 16), 0))
    source = jnp.where(place < 2 * CAP, -1, 4 * (column & 1) + place - 2 * CAP)
    out = dot(bits(iota((n_dst * block, 16), 1) == source), jnp.concatenate([dec, jnp.zeros_like(dec)], axis=0))
    back = (((0,), (0,)), ((), ()))
    out = out + lax.dot_general(keep_ref[...], slots_ref[...], back, preferred_element_type=F32)
    send_ref[...] = out.astype(BF).reshape(send_ref.shape)


def combine_kernel(got_ref, comb_ref, shared_ref, hid_ref, send_ref, dec_ref):
    r = lax.axis_index("req")
    b = lax.axis_index("blk")
    n_src, _, slice_w = got_ref.shape
    n_dst, pre_n, _ = send_ref.shape
    col_n = n_dst * pre_n
    slots = got_ref[...].reshape(n_src * 16, slice_w)
    total = lax.dot_general(comb_ref[...], slots, (((0,), (0,)), ((), ())), preferred_element_type=F32)
    total = total[:col_n]
    first = rounded(total)
    shared = shared_ref[...].astype(F32)
    for d in range(n_dst):
        rows = slice(d * pre_n, (d + 1) * pre_n)
        send_ref[d] = jnp.concatenate(
            [first[rows], total[rows] - first[rows], shared[rows]], axis=1
        ).astype(BF)
    line = iota((8, n_src * 16), 0)
    col = iota((8, n_src * 16), 1)
    pick = jnp.logical_and((col & 15) == 12 + (line & 3), ((col >> 4) & 1) == line >> 2)
    moe = dot(bits(pick), slots)
    dec_ref[...] = (hid_ref[2 * r + (b & 1)].astype(F32) + moe).astype(BF)


def finish_kernel(got_ref, res_ref, own_ref, other_ref, out_ref, dec_ref):
    b = lax.axis_index("blk")
    n_src = got_ref.shape[0]
    slice_w = out_ref.shape[1] // n_src
    got = [got_ref[s].astype(F32) for s in range(n_src)]
    total = jnp.concatenate([g[:, :slice_w] + g[:, slice_w : 2 * slice_w] for g in got], axis=1)
    for g in got:
        total = total + g[:, 2 * slice_w :]
    out_ref[...] = (res_ref[...].astype(F32) + total).astype(BF)

    def flat(ref):
        folded = ref[...].astype(F32)
        return jnp.concatenate([folded[j : j + 1] for j in range(n_src)], axis=1)

    own, other = flat(own_ref), flat(other_ref)
    even = (b & 1) == 0
    dec_ref[...] = jnp.concatenate(
        [jnp.where(even, own, other), jnp.where(even, other, own)], axis=0
    ).astype(BF)


def bucket_sizes(n_slot):
    return tuple(range(n_slot // 2, n_slot + 1, 32))


def call(kernel, outs, args, flops, moved, specs=None, scratch=(), room=16 << 20):
    return pl.pallas_call(
        kernel,
        out_shape=outs,
        in_specs=specs or [VMEM] * len(args),
        out_specs=jax.tree.map(lambda _: VMEM, outs),
        scratch_shapes=scratch,
        cost_estimate=pl.CostEstimate(flops=flops, bytes_accessed=moved, transcendentals=0),
        compiler_params=pltpu.CompilerParams(vmem_limit_bytes=room),
    )(*args)


def local(
    prefill_resid,
    prefill_routes,
    prefill_scores,
    decode_resid,
    queries,
    latent_cache,
    new_latent,
    cache_lengths,
    decode_routes,
    decode_scores,
    norm_gain,
    absorb_key,
    absorb_value,
    out_proj,
    expert_gate,
    expert_up,
    expert_down,
    shared_gate,
    shared_up,
    shared_down,
):
    req_n = lax.axis_size("req")
    blk_n = lax.axis_size("blk")
    pre_n, width = prefill_resid.shape
    slice_w = width // req_n
    col_n = pre_n * req_n
    part_w = absorb_key.shape[2] + 128
    n_slot = 2 * CAP * blk_n
    gain = norm_gain[None]
    sibling = [(i, i ^ 1) for i in range(blk_n)]

    def shape(*dims, dtype=BF):
        return jax.ShapeDtypeStruct(dims, dtype)

    with jax.named_scope("start"):
        sources = (
            queries,
            absorb_key,
            prefill_resid,
            gain,
            prefill_routes,
            prefill_scores,
            decode_routes,
            decode_scores,
            new_latent,
            cache_lengths,
            jnp.swapaxes(latent_cache, 1, 2),
        )
        held = [pltpu.VMEM(a.shape, a.dtype) for a in sources]
        held[9] = pltpu.SMEM(cache_lengths.shape, cache_lengths.dtype)
        sent = call(
            start_kernel,
            shape(req_n, pre_n, width + 128 + part_w),
            tuple(pltpu.with_memory_space_constraint(a, pltpu.HBM) for a in sources),
            10**8,
            4 * 10**6,
            specs=[pl.BlockSpec(memory_space=pltpu.HBM)] * len(sources),
            scratch=held + [pltpu.SemaphoreType.DMA((len(sources),))],
        )
        got = exchange(sent, "req")
    with jax.named_scope("route"):
        sent, cols, comb, decw = call(
            route_kernel,
            (
                shape(blk_n, 16, slice_w),
                shape(col_n, width),
                shape(blk_n * 16, 128),
                shape(16, 128, dtype=F32),
            ),
            (got,),
            10**7,
            10**6,
        )
        got = exchange(sent, "blk")
    with jax.named_scope("heads"):
        sent, keep, info = call(
            head_kernel,
            (
                shape(req_n, n_slot + HEAD, slice_w),
                shape(n_slot, blk_n * 16),
                shape(8, 128, dtype=I32),
            ),
            (got, absorb_value, out_proj, decode_resid),
            10**8,
            3 * 10**6,
        )
        index = info[0, 0]

        def by_size(payload, height):
            def branch(size):
                def run(rows):
                    moved = exchange(rows[:, : HEAD + size], "req")
                    return jnp.pad(moved, ((0, 0), (0, height - HEAD - size), (0, 0)))

                return run

            return lax.switch(index, [branch(size) for size in bucket_sizes(n_slot)], payload)

        rows = by_size(sent, n_slot + HEAD + SLACK)
        rows = pltpu.with_memory_space_constraint(rows, pltpu.VMEM)
    with jax.named_scope("hidden"):
        sent = call(sum_kernel, shape(blk_n, 8, slice_w), (rows,), 10**5, 3 * 10**5)
        got = exchange(sent, "blk")
    with jax.named_scope("experts"):
        streamed = [
            jnp.swapaxes(expert_up, 1, 2),
            expert_down,
            shared_gate.T,
            shared_up.T,
            shared_down,
        ]
        sent, shared, hidden = call(
            terms_kernel,
            (
                shape(req_n, n_slot + HEAD + SLACK, slice_w),
                shape(col_n, width),
                shape(2 * req_n, 8, slice_w),
            ),
            (got, rows, cols, gain, decw, info, jnp.swapaxes(expert_gate, 1, 2))
            + tuple(pltpu.with_memory_space_constraint(a, pltpu.HBM) for a in streamed),
            8 * 10**9,
            12 * 10**6,
            specs=[VMEM] * 7 + [pl.BlockSpec(memory_space=pltpu.HBM)] * 5,
            scratch=[pltpu.VMEM(a.shape, a.dtype) for a in streamed] + [pltpu.SemaphoreType.DMA((7,))],
            room=24 << 20,
        )
        got = by_size(sent, n_slot + HEAD)
    with jax.named_scope("return"):
        slots, mine, give = call(
            hidden_sum_kernel,
            (shape(n_slot, slice_w), shape(8, slice_w, dtype=F32), shape(8, slice_w)),
            (got,),
            10**6,
            2 * 10**6,
        )
        other = lax.ppermute(give, "blk", sibling)
        sent = call(return_kernel, shape(blk_n, 16, slice_w), (slots, keep, mine, other), 10**8, 10**6)
        got = exchange(sent, "blk")
    with jax.named_scope("combine"):
        sent, own_row = call(
            combine_kernel,
            (shape(req_n, pre_n, 2 * slice_w + width), shape(8, slice_w)),
            (got, comb, shared, hidden),
            10**7,
            10**6,
        )
        other_row = lax.ppermute(own_row, "blk", sibling)
        got = exchange(sent, "req")
    with jax.named_scope("finish"):
        prefill_out, decode_out = call(
            finish_kernel,
            (shape(pre_n, width), shape(2, width)),
            (got, prefill_resid, own_row, other_row),
            10**5,
            10**5,
        )
    return (prefill_out, decode_out)


def solution(mesh):
    return jax.shard_map(
        local,
        mesh=mesh,
        in_specs=(
            P(("blk", "req"), None),
            P(("blk", "req"), None),
            P(("blk", "req"), None),
            P("req", None),
            P("req", None, None),
            P("req", "blk", None),
            P("req", None),
            P("req"),
            P("req", None),
            P("req", None),
            P(),
            P(),
            P("req", None, None),
            P("req", None, None),
            P("blk", None, "req"),
            P("blk", None, "req"),
            P("blk", "req", None),
            P(None, "req"),
            P(None, "req"),
            P("req", None),
        ),
        out_specs=(P(("blk", "req"), None), P("req", None)),
        check_vma=False,
    )
```

```python
import jax
import jax.numpy as jnp
from jax import lax
from jax.experimental import pallas as pl
from jax.experimental.pallas import tpu as pltpu
from jax.sharding import PartitionSpec as P

NEG = -1e30
ROUTE_SCALE = 2.446
CAP = 6
HEAD = 16
SLACK = 48
BF = jnp.bfloat16
F32 = jnp.float32
I32 = jnp.int32
VMEM = pl.BlockSpec(memory_space=pltpu.VMEM)
SMEM = pl.BlockSpec(memory_space=pltpu.SMEM)


def exchange(payload, axis):
    return lax.all_to_all(payload, axis, 0, 0, tiled=True)


def dot(a, b):
    return jnp.dot(a, b, preferred_element_type=F32)


def dot_t(a, b):
    return lax.dot_general(a, b, (((1,), (1,)), ((), ())), preferred_element_type=F32)


def iota(shape, dim):
    return lax.broadcasted_iota(I32, shape, dim)


def bits(mask):
    return jnp.where(mask, 1.0, 0.0).astype(BF)


def rounded(values):
    return values.astype(BF).astype(F32)


def pieces(values):
    first = rounded(values)
    second = rounded(values - first)
    return [first, second, values - first - second]


def silu_mul(gate, up):
    return (gate * jax.nn.sigmoid(gate) * up).astype(BF)


def slot_of(row):
    place = row & 15
    second = (place >= CAP).astype(I32)
    return row >> 4, place, second, place - CAP * second


def start_kernel(*refs):
    count = (len(refs) - 2) // 2
    sources, out_ref, held, sems = refs[:count], refs[count], refs[count + 1 : -1], refs[-1]
    copies = [pltpu.make_async_copy(s, h, sems.at[n]) for n, (s, h) in enumerate(zip(sources, held))]
    for copy in copies:
        copy.start()
    q_ref, key_ref, res_ref, gain_ref, prt_ref, psc_ref, drt_ref, dsc_ref, new_ref, len_ref, cache_ref = held
    b = lax.axis_index("blk")
    for copy in copies[2:8]:
        copy.wait()
    pre_n, width = res_ref.shape
    n_req, heads, qw = q_ref.shape
    _, nope, latent = key_ref.shape
    positions = cache_ref.shape[2]
    scale = qw ** (-0.5)

    x = res_ref[...].astype(F32)
    mean_square = jnp.mean(x * x, axis=1, keepdims=True)
    rows = x * lax.rsqrt(mean_square + 1e-06) * gain_ref[...]

    def shares(sc):
        return rounded(sc / jnp.sum(sc, axis=1, keepdims=True) * ROUTE_SCALE)

    lane = iota((pre_n, 128), 1)
    row = iota((pre_n, 128), 0)
    top = prt_ref.shape[1]
    pr, ps = prt_ref[...].astype(F32), shares(psc_ref[...])
    dr, ds = drt_ref[...].astype(F32), shares(dsc_ref[...])
    meta = jnp.zeros((pre_n, 128), F32)
    for k in range(top):
        meta = jnp.where(lane == k, pr[:, k : k + 1], meta)
        meta = jnp.where(lane == top + k, ps[:, k : k + 1], meta)
        for i in range(n_req):
            at = jnp.logical_and(row == 2 * i, lane == 16 + k)
            meta = jnp.where(at, dr[i : i + 1, k : k + 1], meta)
            at = jnp.logical_and(row == 2 * i, lane == 16 + top + k)
            meta = jnp.where(at, ds[i : i + 1, k : k + 1], meta)

    for copy in copies[:2]:
        copy.wait()
    q_all = jnp.concatenate([q_ref[i] for i in range(n_req)], axis=0)
    q_nope = q_all[:, :nope]
    q_rope = q_all[:, nope:]
    q_head = iota((n_req * heads, latent), 0) & (heads - 1)
    q_lat = jnp.zeros((n_req * heads, latent), F32)
    for h in range(heads):
        q_lat = jnp.where(q_head == h, dot(q_nope, key_ref[h]), q_lat)
    q_lat = q_lat.astype(BF)

    for copy in copies[8:]:
        copy.wait()
    fresh_rows = new_ref[...].astype(F32)
    first = b == 0
    parts = []
    for i in range(n_req):
        ql = q_lat[i * heads : (i + 1) * heads]
        qr = q_rope[i * heads : (i + 1) * heads]
        s = (dot(ql, cache_ref[i, :latent, :]) + dot(qr, cache_ref[i, latent:, :])) * scale
        live = b * positions + iota((heads, positions), 1) < len_ref[i]
        s = jnp.where(live, s, NEG)
        new = fresh_rows[i : i + 1]
        fresh = jnp.sum(ql.astype(F32) * new[:, :latent], axis=1, keepdims=True)
        fresh = (fresh + jnp.sum(qr.astype(F32) * new[:, latent:], axis=1, keepdims=True)) * scale
        fresh = jnp.where(first, fresh, NEG)
        peak = jnp.maximum(jnp.max(s, axis=1, keepdims=True), fresh)
        expo = jnp.where(live, jnp.exp(s - peak), 0.0)
        fresh_w = jnp.where(first, jnp.exp(fresh - peak), 0.0)
        total = jnp.sum(expo, axis=1, keepdims=True) + fresh_w
        summed = dot_t(expo.astype(BF), cache_ref[i, :latent, :]) + rounded(fresh_w) * new[:, :latent]
        mean = summed / jnp.where(total > 0.0, total, 1.0)
        lane_h = iota((heads, 128), 1)
        stats = jnp.zeros((heads, 128), F32)
        for k, piece in enumerate(pieces(peak) + pieces(total)):
            stats = jnp.where(lane_h == k, piece, stats)
        parts.append(jnp.concatenate([mean, stats], axis=1))

    own = heads // out_ref.shape[0]
    for d in range(out_ref.shape[0]):
        att = jnp.concatenate([p[own * d : own * (d + 1)] for p in parts], axis=0)
        out_ref[d] = jnp.concatenate([rows, meta, att], axis=1).astype(BF)


def route_kernel(got_ref, send_ref, cols_ref, comb_ref, decw_ref):
    r = lax.axis_index("req")
    b = lax.axis_index("blk")
    n_src, pre_n, _ = got_ref.shape
    col_n, width = cols_ref.shape
    slice_w = send_ref.shape[2]
    blk_n = send_ref.shape[0]
    experts = 2 * blk_n
    top = 6
    full = jnp.concatenate([got_ref[s].astype(F32) for s in range(n_src)], axis=0)
    cols_ref[...] = full[:, :width].astype(BF)
    meta = full[:, width : width + 128]
    pairs = full[:, width + 128 :]

    expert = iota((col_n, experts), 1).astype(F32)
    named = jnp.zeros((col_n, experts), F32)
    weight = jnp.zeros((col_n, experts), F32)
    for k in range(top):
        hit = meta[:, k : k + 1] == expert
        named = jnp.where(hit, 1.0, named)
        weight = jnp.where(hit, meta[:, top + k : top + k + 1], weight)
    earlier = bits(iota((col_n, col_n), 1) < iota((col_n, col_n), 0))
    rank = dot(earlier, named.astype(BF))
    value = jnp.where(named > 0.0, rank + 1.0, 0.0)

    n_row = blk_n * 16
    column, place, second, slot = slot_of(iota((n_row, experts), 0))
    picks = jnp.logical_and(iota((n_row, experts), 1) == 2 * column + second, place < 2 * CAP)
    picks = bits(picks)
    rest = jnp.zeros((128 - col_n, experts), F32)
    value = dot_t(picks, jnp.concatenate([value, rest], axis=0).astype(BF))
    weight = dot_t(picks, jnp.concatenate([weight, rest], axis=0).astype(BF))
    row = iota((n_row, 128), 0)
    lane = iota((n_row, 128), 1)
    _, _, _, slot = slot_of(row)
    chosen = value == (slot + 1).astype(F32)
    comb_ref[...] = jnp.where(chosen, weight, 0.0).astype(BF)
    carried = jnp.logical_and(lane >= col_n, row == (lane & (col_n - 1)) * 16 + 11 + (lane >> 5))
    mine = cols_ref[:, pl.ds(pl.multiple_of(r * slice_w, slice_w), slice_w)]
    line = iota((col_n, experts), 0)
    lane = iota((col_n, experts), 1)
    tail = jnp.zeros((col_n, slice_w - 128), F32)
    for k in range(2):
        count = dot_t(bits(lane == 2 * line + k), named.astype(BF))
        count = jnp.sum(count, axis=1, keepdims=True)
        tail = jnp.where(iota(tail.shape, 1) == k, count, tail)
    last = jnp.concatenate([pairs[:, 2 * slice_w :], tail], axis=1)
    data = jnp.concatenate(
        [mine, pairs[:, :slice_w].astype(BF), pairs[:, slice_w : 2 * slice_w].astype(BF), last.astype(BF)],
        axis=0,
    )
    moved = dot(bits(jnp.logical_or(chosen, carried)), data).astype(BF)
    send_ref[...] = moved.reshape(send_ref.shape)

    lane = iota((col_n, 128), 1)
    dec = jnp.zeros((col_n, 128), F32)
    for k in range(2):
        own = (2 * b + k).astype(F32)
        got = jnp.zeros((col_n, 1), F32)
        for j in range(top):
            hit = meta[:, 16 + j : 17 + j] == own
            got = jnp.where(hit, meta[:, 16 + top + j : 17 + top + j], got)
        dec = jnp.where(lane == k, got, dec)
    even = bits(iota((col_n // 2, col_n), 1) == 2 * iota((col_n // 2, col_n), 0))
    decw_ref[...] = dot(even, dec.astype(BF))


def head_kernel(got_ref, val_ref, proj_ref, res_ref, send_ref, keep_ref, info_ref):
    r = lax.axis_index("req")
    b = lax.axis_index("blk")
    n_src, block, slice_w = got_ref.shape
    n_dst, n_out, _ = send_ref.shape
    n_slot = n_out - HEAD
    n_col = n_src * block
    got = got_ref[...].reshape(n_col, slice_w)
    line = iota((3 * n_src, n_src * block), 0)
    part = iota((3 * n_src, n_src * block), 1) == (line & (n_src - 1)) * block + 12 + (line >> 5)
    part = dot(bits(part), got)
    stats = part[2 * n_src :]

    count = stats[:, 128:]
    earlier = bits(iota((n_src, n_src), 1) < iota((n_src, n_src), 0))
    before = dot(earlier, count.astype(BF))
    spread = bits(iota((n_src, n_col), 1) >> 4 == iota((n_src, n_col), 0))
    table = jnp.concatenate([before, count], axis=1).astype(BF)
    table = lax.dot_general(table, spread, (((0,), (0,)), ((), ())), preferred_element_type=F32)
    used = jnp.sum(count, axis=0, keepdims=True)
    first_n = used[:, 0:1]
    column, place, second, slot = slot_of(iota((1, n_col), 1))
    slot = slot.astype(F32)
    width = count.shape[1]
    target = jnp.where(second == 1, table[1:2] + first_n, table[0:1]) + slot
    named = jnp.where(second == 1, table[width + 1 : width + 2], table[width : width + 1])
    target = jnp.where(jnp.logical_and(slot < named, place < 2 * CAP), target, -1.0)
    keep = bits(iota((n_slot, n_col), 0).astype(F32) == target)
    keep_ref[...] = keep
    slots = dot(keep, got).astype(BF)
    for d in range(n_dst):
        send_ref[d, HEAD:, :] = slots
    both = first_n + used[:, 1:2]
    index = jnp.zeros((1, 1), F32)
    for size in bucket_sizes(n_slot)[:-1]:
        index = index + jnp.where(both > size, 1.0, 0.0)
    lane = iota(info_ref.shape, 1)
    info_ref[...] = jnp.where(lane == 0, index, jnp.where(lane == 1, first_n, 0.0)).astype(I32)

    peak = stats[:, 0:1] + stats[:, 1:2] + stats[:, 2:3]
    total = stats[:, 3:4] + stats[:, 4:5] + stats[:, 5:6]
    share = total * jnp.exp(peak - jnp.max(peak, axis=0, keepdims=True))
    whole = jnp.sum(share, axis=0, keepdims=True)
    low = jnp.sum(part[:n_src] * share, axis=0, keepdims=True) / whole
    high = jnp.sum(part[n_src : 2 * n_src] * share, axis=0, keepdims=True) / whole
    o_latent = jnp.broadcast_to(jnp.concatenate([low, high], axis=1), (8, 2 * slice_w)).astype(BF)
    head = b & 1
    request = b >> 1
    head_value = dot(o_latent, val_ref[head]).astype(BF)
    projected = dot(head_value, proj_ref[head])[0:1]
    resid = res_ref[...].astype(F32)
    resid = jnp.where(iota(resid.shape, 0) == (request & 1), resid, 0.0)
    resid = jnp.sum(resid, axis=0, keepdims=True)
    owner = jnp.logical_and(request >> 1 == r, head == 0)
    projected = projected + jnp.where(owner, resid, 0.0)
    folded = jnp.concatenate(
        [projected[:, slice_w * j : slice_w * (j + 1)] for j in range(8)], axis=0
    )
    folded = jnp.concatenate([folded, jnp.zeros((HEAD - 8, slice_w), F32)], axis=0).astype(BF)
    for d in range(n_dst):
        send_ref[d, :HEAD, :] = folded


def sum_kernel(got_ref, send_ref):
    n_src = got_ref.shape[0]
    total = got_ref[0, :HEAD, :].astype(F32)
    for s in range(1, n_src):
        total = total + got_ref[s, :HEAD, :].astype(F32)
    total = total[:8].astype(BF)
    for d in range(send_ref.shape[0]):
        send_ref[d] = total


def terms_kernel(
    got_ref,
    rows_ref,
    cols_ref,
    gain_ref,
    decw_ref,
    info_ref,
    gate_ref,
    up_ref,
    down_ref,
    sg_ref,
    su_ref,
    sd_ref,
    out_ref,
    shared_ref,
    hid_ref,
):
    b = lax.axis_index("blk")
    n_src, fold, slice_w = got_ref.shape
    dec_n = n_src // 2
    n_line = fold * dec_n
    got = got_ref[...].reshape(n_src * fold, slice_w)
    line = iota((n_line, n_src * fold), 0)
    col = iota((n_line, n_src * fold), 1)
    pick = jnp.logical_and(col >> 4 == (line & (dec_n - 1)), (col & 7) == line >> 4)
    hidden = dot(bits(pick), got).astype(BF)
    wide = hidden.astype(F32)
    chunks = [wide[j * dec_n : (j + 1) * dec_n] for j in range(fold)]
    square = sum(jnp.sum(c * c, axis=1, keepdims=True) for c in chunks)
    factor = lax.rsqrt(square / (fold * slice_w) + 1e-06)
    normed = [
        (c * factor * gain_ref[:, j * slice_w : (j + 1) * slice_w]).astype(BF)
        for j, c in enumerate(chunks)
    ]

    col_n = cols_ref.shape[0]
    x = jnp.concatenate([cols_ref[...], jnp.concatenate(normed, axis=1)], axis=0)
    act = silu_mul(dot_t(x, sg_ref[...]), dot_t(x, su_ref[...]))
    shared = dot(act, sd_ref[...])
    shared_ref[...] = shared[:col_n].astype(BF)
    mine = jnp.where(iota((dec_n, 1), 0) == (b >> 1), 1.0, 0.0) * jnp.where((b & 1) == 0, 1.0, 0.0)
    dec = [mine * shared[col_n:, j * slice_w : (j + 1) * slice_w] for j in range(fold)]

    n_dst, n_row, _ = out_ref.shape
    half = (n_row - HEAD - SLACK) // 2
    first_n = jnp.max(jnp.where(iota(info_ref.shape, 1) == 1, info_ref[...], 0).astype(F32)).astype(I32)
    start = pl.multiple_of(HEAD + ((first_n >> 4) << 4), 16)
    for k in range(gate_ref.shape[0]):
        size = half if k == 0 else half + SLACK
        span = pl.ds(HEAD, size) if k == 0 else pl.ds(start, size)
        gate, up = 0.0, 0.0
        for s in range(n_dst):
            x = jnp.concatenate([rows_ref[s, span, :], normed[s]], axis=0)
            lanes = slice(s * slice_w, (s + 1) * slice_w)
            gate = gate + dot_t(x, gate_ref[k, :, lanes])
            up = up + dot_t(x, up_ref[k, :, lanes])
        act = silu_mul(gate, up)
        later = iota((size, slice_w), 0) + (start - HEAD) >= first_n
        for d in range(n_dst):
            out = dot(act, down_ref[k, :, d * slice_w : (d + 1) * slice_w])
            dec[d] = dec[d] + decw_ref[:, k : k + 1] * out[size:]
            rows = out[:size]
            if k == 1:
                rows = jnp.where(later, rows, out_ref[d, span, :].astype(F32))
            out_ref[d, span, :] = rows.astype(BF)

    line = iota((n_line, n_line), 0)
    col = iota((n_line, n_line), 1)
    swap = bits(col == (line & 7) * dec_n + (line >> 3))
    turned = dot(swap, jnp.concatenate([d.astype(BF) for d in dec], axis=0)).astype(BF)
    out_ref[:, :HEAD, :] = turned.reshape(n_dst, 16, slice_w)
    hid_ref[...] = dot(swap, hidden).reshape(hid_ref.shape).astype(BF)


def hidden_sum_kernel(got_ref, slots_ref, keep_ref, give_ref):
    b = lax.axis_index("blk")
    n_src = got_ref.shape[0]
    total = got_ref[0].astype(F32)
    for s in range(1, n_src):
        total = total + got_ref[s].astype(F32)
    slots_ref[...] = total[HEAD:].astype(BF)
    dec = total[:HEAD]
    low = jnp.concatenate([dec[0:4], dec[8:12]], axis=0)
    high = jnp.concatenate([dec[4:8], dec[12:16]], axis=0)
    even = (b & 1) == 0
    keep_ref[...] = jnp.where(even, low, high)
    give_ref[...] = jnp.where(even, high, low).astype(BF)


def return_kernel(slots_ref, keep_ref, mine_ref, other_ref, send_ref):
    n_dst, block, _ = send_ref.shape
    dec = (mine_ref[...] + other_ref[...].astype(F32)).astype(BF)
    column, place, second, slot = slot_of(iota((n_dst * block, 16), 0))
    source = jnp.where(place < 2 * CAP, -1, 4 * (column & 1) + place - 2 * CAP)
    out = dot(bits(iota((n_dst * block, 16), 1) == source), jnp.concatenate([dec, jnp.zeros_like(dec)], axis=0))
    back = (((0,), (0,)), ((), ()))
    out = out + lax.dot_general(keep_ref[...], slots_ref[...], back, preferred_element_type=F32)
    send_ref[...] = out.astype(BF).reshape(send_ref.shape)


def combine_kernel(got_ref, comb_ref, shared_ref, hid_ref, send_ref, dec_ref):
    r = lax.axis_index("req")
    b = lax.axis_index("blk")
    n_src, _, slice_w = got_ref.shape
    n_dst, pre_n, _ = send_ref.shape
    col_n = n_dst * pre_n
    slots = got_ref[...].reshape(n_src * 16, slice_w)
    total = lax.dot_general(comb_ref[...], slots, (((0,), (0,)), ((), ())), preferred_element_type=F32)
    total = total[:col_n]
    first = rounded(total)
    shared = shared_ref[...].astype(F32)
    for d in range(n_dst):
        rows = slice(d * pre_n, (d + 1) * pre_n)
        send_ref[d] = jnp.concatenate(
            [first[rows], total[rows] - first[rows], shared[rows]], axis=1
        ).astype(BF)
    line = iota((8, n_src * 16), 0)
    col = iota((8, n_src * 16), 1)
    pick = jnp.logical_and((col & 15) == 12 + (line & 3), ((col >> 4) & 1) == line >> 2)
    moe = dot(bits(pick), slots)
    dec_ref[...] = (hid_ref[2 * r + (b & 1)].astype(F32) + moe).astype(BF)


def finish_kernel(got_ref, res_ref, own_ref, other_ref, out_ref, dec_ref):
    b = lax.axis_index("blk")
    n_src = got_ref.shape[0]
    slice_w = out_ref.shape[1] // n_src
    got = [got_ref[s].astype(F32) for s in range(n_src)]
    total = jnp.concatenate([g[:, :slice_w] + g[:, slice_w : 2 * slice_w] for g in got], axis=1)
    for g in got:
        total = total + g[:, 2 * slice_w :]
    out_ref[...] = (res_ref[...].astype(F32) + total).astype(BF)

    def flat(ref):
        folded = ref[...].astype(F32)
        return jnp.concatenate([folded[j : j + 1] for j in range(n_src)], axis=1)

    own, other = flat(own_ref), flat(other_ref)
    even = (b & 1) == 0
    dec_ref[...] = jnp.concatenate(
        [jnp.where(even, own, other), jnp.where(even, other, own)], axis=0
    ).astype(BF)


def bucket_sizes(n_slot):
    return tuple(range(n_slot // 2, n_slot + 1, 32))


def call(kernel, outs, args, flops, moved, specs=None, scratch=()):
    return pl.pallas_call(
        kernel,
        out_shape=outs,
        in_specs=specs or [VMEM] * len(args),
        out_specs=jax.tree.map(lambda _: VMEM, outs),
        scratch_shapes=scratch,
        cost_estimate=pl.CostEstimate(flops=flops, bytes_accessed=moved, transcendentals=0),
        compiler_params=pltpu.CompilerParams(vmem_limit_bytes=16 << 20),
    )(*args)


def local(
    prefill_resid,
    prefill_routes,
    prefill_scores,
    decode_resid,
    queries,
    latent_cache,
    new_latent,
    cache_lengths,
    decode_routes,
    decode_scores,
    norm_gain,
    absorb_key,
    absorb_value,
    out_proj,
    expert_gate,
    expert_up,
    expert_down,
    shared_gate,
    shared_up,
    shared_down,
):
    req_n = lax.axis_size("req")
    blk_n = lax.axis_size("blk")
    pre_n, width = prefill_resid.shape
    slice_w = width // req_n
    col_n = pre_n * req_n
    part_w = absorb_key.shape[2] + 128
    n_slot = 2 * CAP * blk_n
    gain = norm_gain[None]
    sibling = [(i, i ^ 1) for i in range(blk_n)]

    def shape(*dims, dtype=BF):
        return jax.ShapeDtypeStruct(dims, dtype)

    with jax.named_scope("start"):
        sources = (
            queries,
            absorb_key,
            prefill_resid,
            gain,
            prefill_routes,
            prefill_scores,
            decode_routes,
            decode_scores,
            new_latent,
            cache_lengths,
            jnp.swapaxes(latent_cache, 1, 2),
        )
        held = [pltpu.VMEM(a.shape, a.dtype) for a in sources]
        held[9] = pltpu.SMEM(cache_lengths.shape, cache_lengths.dtype)
        sent = call(
            start_kernel,
            shape(req_n, pre_n, width + 128 + part_w),
            tuple(pltpu.with_memory_space_constraint(a, pltpu.HBM) for a in sources),
            10**8,
            4 * 10**6,
            specs=[pl.BlockSpec(memory_space=pltpu.HBM)] * len(sources),
            scratch=held + [pltpu.SemaphoreType.DMA((len(sources),))],
        )
        got = exchange(sent, "req")
    with jax.named_scope("route"):
        sent, cols, comb, decw = call(
            route_kernel,
            (
                shape(blk_n, 16, slice_w),
                shape(col_n, width),
                shape(blk_n * 16, 128),
                shape(16, 128, dtype=F32),
            ),
            (got,),
            10**7,
            10**6,
        )
        got = exchange(sent, "blk")
    with jax.named_scope("heads"):
        sent, keep, info = call(
            head_kernel,
            (
                shape(req_n, n_slot + HEAD, slice_w),
                shape(n_slot, blk_n * 16),
                shape(8, 128, dtype=I32),
            ),
            (got, absorb_value, out_proj, decode_resid),
            10**8,
            3 * 10**6,
        )
        index = info[0, 0]

        def by_size(payload, height):
            def branch(size):
                def run(rows):
                    moved = exchange(rows[:, : HEAD + size], "req")
                    return jnp.pad(moved, ((0, 0), (0, height - HEAD - size), (0, 0)))

                return run

            return lax.switch(index, [branch(size) for size in bucket_sizes(n_slot)], payload)

        rows = by_size(sent, n_slot + HEAD + SLACK)
        rows = pltpu.with_memory_space_constraint(rows, pltpu.VMEM)
    with jax.named_scope("hidden"):
        sent = call(sum_kernel, shape(blk_n, 8, slice_w), (rows,), 10**10, 5 * 10**7)
        got = exchange(sent, "blk")
    with jax.named_scope("experts"):
        sent, shared, hidden = call(
            terms_kernel,
            (
                shape(req_n, n_slot + HEAD + SLACK, slice_w),
                shape(col_n, width),
                shape(2 * req_n, 8, slice_w),
            ),
            (
                got,
                rows,
                cols,
                gain,
                decw,
                info,
                jnp.swapaxes(expert_gate, 1, 2),
                jnp.swapaxes(expert_up, 1, 2),
                expert_down,
                shared_gate.T,
                shared_up.T,
                shared_down,
            ),
            8 * 10**9,
            12 * 10**6,
        )
        got = by_size(sent, n_slot + HEAD)
    with jax.named_scope("return"):
        slots, mine, give = call(
            hidden_sum_kernel,
            (shape(n_slot, slice_w), shape(8, slice_w, dtype=F32), shape(8, slice_w)),
            (got,),
            10**6,
            2 * 10**6,
        )
        other = lax.ppermute(give, "blk", sibling)
        sent = call(return_kernel, shape(blk_n, 16, slice_w), (slots, keep, mine, other), 10**8, 10**6)
        got = exchange(sent, "blk")
    with jax.named_scope("combine"):
        sent, own_row = call(
            combine_kernel,
            (shape(req_n, pre_n, 2 * slice_w + width), shape(8, slice_w)),
            (got, comb, shared, hidden),
            10**7,
            10**6,
        )
        other_row = lax.ppermute(own_row, "blk", sibling)
        got = exchange(sent, "req")
    with jax.named_scope("finish"):
        prefill_out, decode_out = call(
            finish_kernel,
            (shape(pre_n, width), shape(2, width)),
            (got, prefill_resid, own_row, other_row),
            10**5,
            10**5,
        )
    return (prefill_out, decode_out)


def solution(mesh):
    return jax.shard_map(
        local,
        mesh=mesh,
        in_specs=(
            P(("blk", "req"), None),
            P(("blk", "req"), None),
            P(("blk", "req"), None),
            P("req", None),
            P("req", None, None),
            P("req", "blk", None),
            P("req", None),
            P("req"),
            P("req", None),
            P("req", None),
            P(),
            P(),
            P("req", None, None),
            P("req", None, None),
            P("blk", None, "req"),
            P("blk", None, "req"),
            P("blk", "req", None),
            P(None, "req"),
            P(None, "req"),
            P("req", None),
        ),
        out_specs=(P(("blk", "req"), None), P("req", None)),
        check_vma=False,
    )
```
